128 devices in a mesh: req: 32 (over x, z, core), tp: 4 (over y).
Axes of the slice: x: 4, y: 4, z: 4, core: 2. Of those that a mesh axis runs over, the one named last changes fastest.
Arguments:
- tokens: bfloat16 [1024, 2048], P('req'), may hold values from -6 to 6
- deal_order: int32 [1024], replicated, may hold values from 0 to 1023, as said below
- page_table: int32 [1024, 6], P('req'), may hold values from 0 to 1343, as said below
- lengths: int32 [1024], P('req'), may hold values from 1 to 768, as said below
- qkv_weight: bfloat16 [2048, 3, 2048], P(None, None, 'tp'), may hold values from -0.125 to 0.125
- out_weight: bfloat16 [2048, 2048], P('tp'), may hold values from -0.125 to 0.125
- up_weight: bfloat16 [2048, 4096], P(None, 'tp'), may hold values from -0.125 to 0.125
- down_weight: bfloat16 [4096, 2048], P('tp'), may hold values from -0.09375 to 0.09375
- key_cache: bfloat16 [2, 1344, 128, 2048], P(None, 'req', None, 'tp')
- value_cache: bfloat16 [2, 1344, 128, 2048], P(None, 'req', None, 'tp'), may hold values from -6 to 6
- attn_norm: float32 [2, 2048], replicated
- mlp_norm: float32 [2, 2048], replicated
Outputs:
- output: bfloat16 [1024, 2048], P('req')
The draws below stay inside these ranges and needn't reach their ends.
Inputs may be any that keep to these rules, and one draw needn't show every extreme that they name: `deal_order`: A permutation: every request is placed in exactly one slot. Of the 32 requests in the slots s // 32 = d of one block d, at most 2 come from one source block of rows r // 32 = j, and some pair of blocks has exactly 2. `page_table`: row s holds the pages of the request in dealt slot s: its first ceil(lengths[s] / 128) entries are pages of the block s // 32 * 42 to s // 32 * 42 + 41, no page serves two slots, and the remaining entries repeat the row's first page. `lengths`: A request fills at most 6 pages; the slots s // 32 = d of one block d fill at most 42 pages together, and some block fills exactly that many.
All inputs are finite; a program needn't handle non-finite values.
Results may differ from the reference program's by a relative error of at most 0.034.
Values may be sent and summed in bfloat16 or wider, within the bound.
No kernel may reach another device: no remote copies, remote signals or barrier semaphores. Data moves between devices by JAX's collectives and lax.ppermute only.
A program may use at most 448 MiB of HBM per device.

```python
import math
import jax
import jax.numpy as jnp
from jax import lax

D = 2048
HEADS = 16
HD = 128
FF = 4096
LAYERS = 2
PAGE = 128
MAXP = 6
R_DEV = 32
PAGES_DEV = 42
REQUESTS = 1024
POOL = 1344
CAP = 2


def draw_deal_order(key, part):
    dev_count = REQUESTS // R_DEV
    group_count = R_DEV // CAP
    key_label, key_offset, key_local, key_slot = jax.random.split(jax.random.fold_in(key, 505), 4)
    relabel = jax.random.permutation(key_label, dev_count).astype(jnp.int32)
    unlabel = jnp.zeros((dev_count,), jnp.int32).at[relabel].set(jnp.arange(dev_count, dtype=jnp.int32))
    offsets = jax.random.permutation(key_offset, dev_count).astype(jnp.int32)[:group_count]
    source = unlabel[(relabel[:, None] + offsets[None, :]) % dev_count]
    local_perm = jax.vmap(lambda one_key: jax.random.permutation(one_key, R_DEV))(jax.random.split(key_local, dev_count)).astype(jnp.int32)
    source_slot = jnp.repeat(source, CAP, axis=1)
    column = jnp.arange(R_DEV, dtype=jnp.int32)
    local_rows = jnp.take_along_axis(local_perm[source_slot.reshape(-1)].reshape(dev_count, R_DEV, R_DEV), jnp.broadcast_to(column[None, :, None], (dev_count, R_DEV, 1)), axis=2)[:, :, 0]
    base = source_slot * R_DEV + local_rows
    slot_perm = jax.vmap(lambda one_key: jax.random.permutation(one_key, R_DEV))(jax.random.split(key_slot, dev_count)).astype(jnp.int32)
    dealt = jnp.take_along_axis(base, slot_perm, axis=1)
    return dealt.reshape(REQUESTS).astype(jnp.int32)


def page_layout(key):
    dev_count = REQUESTS // R_DEV
    salted = jax.random.fold_in(key, 101)
    key_full, key_extra, key_first, key_second, key_tail, key_order = jax.random.split(salted, 6)
    extra_cap = PAGES_DEV - R_DEV
    dev_ids = jnp.arange(dev_count, dtype=jnp.int32)
    slot_ids = jnp.arange(R_DEV, dtype=jnp.int32)
    full_dev = jax.random.randint(key_full, (), 0, dev_count)
    extras = jax.random.randint(key_extra, (dev_count,), 0, extra_cap + 1)
    extras = jnp.where(dev_ids == full_dev, extra_cap, extras)
    first_req = jax.random.randint(key_first, (dev_count,), 0, R_DEV)
    second_req = (first_req + jax.random.randint(key_second, (dev_count,), 1, R_DEV)) % R_DEV
    take_first = jnp.minimum(extras, MAXP - 1)
    take_second = extras - take_first
    page_count = 1 + jnp.where(slot_ids[None, :] == first_req[:, None], take_first[:, None], 0)
    page_count = page_count + jnp.where(slot_ids[None, :] == second_req[:, None], take_second[:, None], 0)
    tail_len = jax.random.randint(key_tail, (dev_count, R_DEV), 1, PAGE + 1)
    longest = (dev_ids[:, None] == full_dev) & (slot_ids[None, :] == first_req[:, None])
    tail_len = jnp.where(longest, PAGE, tail_len)
    token_counts = (page_count - 1) * PAGE + tail_len
    order_keys = jax.random.split(key_order, dev_count)
    page_order = jax.vmap(lambda one_key: jax.random.permutation(one_key, PAGES_DEV))(order_keys)
    first_page = jnp.cumsum(page_count, axis=1) - page_count
    slot_span = jnp.arange(MAXP, dtype=jnp.int32)
    offset = jnp.where(slot_span[None, None, :] < page_count[:, :, None], slot_span[None, None, :], 0)
    pick_index = (first_page[:, :, None] + offset).reshape(dev_count, R_DEV * MAXP)
    chosen = jnp.take_along_axis(page_order, pick_index, axis=1) + dev_ids[:, None] * PAGES_DEV
    return (chosen.reshape(REQUESTS, MAXP).astype(jnp.int32), token_counts.reshape(REQUESTS).astype(jnp.int32))


def draw_page_table(key, part):
    return page_layout(key)[0]


def draw_lengths(key, part):
    return page_layout(key)[1]


def draw_key_cache(key, part):
    key_one = jax.random.fold_in(jax.random.fold_in(key, 202), 0)
    normal_part = jnp.clip(jax.random.normal(key_one, (LAYERS, POOL, PAGE, D), jnp.float32), -5.0, 5.0)
    return normal_part.astype(jnp.bfloat16)


def draw_norm_rows(key, salt):
    key_one, key_two = jax.random.split(jax.random.fold_in(key, salt), 2)
    ramp_up = jnp.exp(jnp.log(3.0) * jnp.arange(D, dtype=jnp.float32) / D)
    gain_row = 0.6 * ramp_up * jax.random.uniform(key_one, (D,), jnp.float32, 0.8, 1.25)
    bias_row = 0.3 * jax.random.normal(key_two, (D,), jnp.float32)
    return jnp.stack([gain_row, bias_row]).astype(jnp.float32)


def draw_attn_norm(key, part):
    return draw_norm_rows(key, 303)


def draw_mlp_norm(key, part):
    return draw_norm_rows(key, 404)


def level_of(stream_key, dims, cuts, smallest, top_value):
    factor_of = 1.0
    for dim, blocks in cuts:
        draws = jax.random.uniform(jax.random.fold_in(jax.random.fold_in(stream_key, 6), dim), (blocks,), jnp.float32, smallest / len(cuts), top_value / len(cuts))
        factor_of = factor_of * jnp.repeat(jnp.exp(draws), dims[dim] // blocks).reshape((-1,) + (1,) * (len(dims) - 1 - dim))
    return factor_of


def normal_values(rng, extent, deviation, most, cuts=(), kind=jnp.bfloat16):
    loudness = level_of(rng, extent, cuts, -0.22, 0.18) if cuts else 1.0
    drawn = jax.random.normal(rng, extent, jnp.float32) * deviation * loudness
    return jnp.minimum(jnp.maximum(drawn, -most), most).astype(kind)


def setup_inputs(seed: int = 0) -> dict:
    key_list = jax.random.split(jax.random.key(seed), 13)
    tokens = normal_values(key_list[0], (REQUESTS, D), 1.0, 6.0, ((0, 32),))
    deal_order = draw_deal_order(jax.random.fold_in(key_list[12], 71), 0)
    page_table = draw_page_table(jax.random.fold_in(key_list[12], 71), 0)
    lengths = draw_lengths(jax.random.fold_in(key_list[12], 71), 0)
    qkv_weight = normal_values(key_list[4], (D, 3, D), D ** -0.5, 0.125, ((2, 4),))
    out_weight = normal_values(key_list[5], (D, D), D ** -0.5, 0.125, ((0, 4),))
    up_weight = normal_values(key_list[6], (D, FF), D ** -0.5, 0.125, ((1, 4),))
    down_weight = normal_values(key_list[7], (FF, D), FF ** -0.5, 0.09375, ((0, 4),))
    key_cache = draw_key_cache(jax.random.fold_in(key_list[12], 71), 0)
    value_cache = normal_values(key_list[9], (LAYERS, POOL, PAGE, D), 1.0, 6.0, ((1, 32), (3, 4)))
    attn_norm = draw_attn_norm(jax.random.fold_in(key_list[12], 71), 0)
    mlp_norm = draw_mlp_norm(jax.random.fold_in(key_list[12], 71), 0)
    return {"tokens": tokens, "deal_order": deal_order, "page_table": page_table, "lengths": lengths, "qkv_weight": qkv_weight, "out_weight": out_weight, "up_weight": up_weight, "down_weight": down_weight, "key_cache": key_cache, "value_cache": value_cache, "attn_norm": attn_norm, "mlp_norm": mlp_norm}


epsilon = 1e-06

def layer_norm(row_total, gain_bias):
    row_mean = lax.optimization_barrier(jnp.mean(row_total, axis=-1, keepdims=True))
    centered = row_total - row_mean
    row_var = lax.optimization_barrier(jnp.mean(centered * centered, axis=-1, keepdims=True))
    return (centered * lax.rsqrt(row_var + epsilon) * gain_bias[0] + gain_bias[1]).astype(jnp.bfloat16)

def reference(tokens, deal_order, page_table, lengths, qkv_weight, out_weight, up_weight, down_weight, key_cache, value_cache, attn_norm, mlp_norm):
    score_scale = 1.0 / math.sqrt(HD)
    current = tokens[deal_order]
    qkv_flat = qkv_weight.reshape(D, 3 * D)
    span_len = MAXP * PAGE
    for layer_index in range(LAYERS):
        projected = jnp.dot(current, qkv_flat, preferred_element_type=jnp.float32).astype(jnp.bfloat16)
        query_all = projected[:, :D].reshape(REQUESTS, HEADS, HD)
        fresh_keys = projected[:, D:2 * D].reshape(REQUESTS, HEADS, HD)
        fresh_values = projected[:, 2 * D:].reshape(REQUESTS, HEADS, HD)
        key_layer = key_cache[layer_index]
        value_layer = value_cache[layer_index]

        def one_request(operands):
            query_row, key_new, value_new, table_row, length = operands
            key_rows = key_layer[table_row].reshape(span_len, HEADS, HD).astype(jnp.float32)
            value_rows = value_layer[table_row].reshape(span_len, HEADS, HD).astype(jnp.float32)
            scores = jnp.einsum('hd,thd->ht', query_row.astype(jnp.float32), key_rows) * score_scale
            position = jnp.arange(span_len, dtype=jnp.int32)
            scores = jnp.where(position[None, :] < length, scores, -jnp.inf)
            own_score = lax.optimization_barrier(jnp.sum(query_row.astype(jnp.float32) * key_new.astype(jnp.float32), axis=-1)) * score_scale
            row_max = jnp.maximum(lax.optimization_barrier(jnp.max(scores, axis=-1)), own_score)
            exp_cache = jnp.exp(scores - row_max[:, None])
            exp_own = jnp.exp(own_score - row_max)
            row_total = lax.optimization_barrier(jnp.sum(exp_cache, axis=-1)) + exp_own
            cache_weights = (exp_cache / row_total[:, None]).astype(jnp.bfloat16).astype(jnp.float32)
            own_weight = (exp_own / row_total).astype(jnp.bfloat16).astype(jnp.float32)
            mixed_cache = jnp.einsum('ht,thd->hd', cache_weights, value_rows)
            attended_row = mixed_cache + own_weight[:, None] * value_new.astype(jnp.float32)
            return attended_row.reshape(D).astype(jnp.bfloat16)
        attended = lax.map(one_request, (query_all, fresh_keys, fresh_values, page_table, lengths))
        attn_sum = jnp.dot(attended, out_weight, preferred_element_type=jnp.float32)
        hidden = layer_norm(current.astype(jnp.float32) + attn_sum, attn_norm)
        up_proj = jnp.dot(hidden, up_weight, preferred_element_type=jnp.float32)
        activated = jax.nn.gelu(up_proj, approximate=True).astype(jnp.bfloat16)
        down_proj = jnp.dot(activated, down_weight, preferred_element_type=jnp.float32)
        current = layer_norm(hidden.astype(jnp.float32) + down_proj, mlp_norm)
    return jnp.zeros_like(current).at[deal_order].set(current)
```

```python
import math

import jax
import jax.numpy as jnp
from jax import lax
from jax.sharding import PartitionSpec as P

HD = 128
CAP = 2
EPS = 1e-6
BF = jnp.bfloat16
F32 = jnp.float32


def layer_norm(row_total, gain_bias):
    row_mean = jnp.mean(row_total, axis=-1, keepdims=True)
    centered = row_total - row_mean
    row_var = jnp.mean(centered * centered, axis=-1, keepdims=True)
    return (centered * lax.rsqrt(row_var + EPS) * gain_bias[0] + gain_bias[1]).astype(BF)


def post_norm(partial_term, residual, gain_bias):
    part = partial_term.astype(BF)
    size = lax.axis_size("tp")
    total = part.astype(F32)
    for step in range(1, size):
        moved = lax.ppermute(part, "tp", [(i, (i + step) % size) for i in range(size)])
        total = total + moved.astype(F32)
    return layer_norm(total + residual.astype(F32), gain_bias)


def deal_maps(deal_order, req_index, rows, blocks):
    here = deal_order.reshape(blocks, rows) - req_index * rows
    row_ids = jnp.arange(rows, dtype=jnp.int32)
    sent = jnp.any(here[:, :, None] == row_ids[None, None, :], axis=1)
    sent_f = sent.astype(F32)
    earlier = (row_ids[:, None] < row_ids[None, :]).astype(F32)
    rank = jnp.dot(sent_f, earlier, precision=lax.Precision.HIGHEST)
    ranks = jnp.arange(CAP, dtype=F32)
    send = (sent[:, None, :] & (rank[:, None, :] == ranks[None, :, None])).astype(BF)
    mine = lax.dynamic_slice_in_dim(deal_order, req_index * rows, rows)
    source = mine // rows
    order = jnp.sum(
        (source[:, None] == source[None, :]) & (mine[None, :] < mine[:, None]), axis=1
    )
    place = source * CAP + order
    take = (place[:, None] == jnp.arange(blocks * CAP, dtype=jnp.int32)[None, :]).astype(BF)
    return send.reshape(blocks * CAP, rows), take


def exchange(rows_here, send, take, blocks):
    width = rows_here.shape[1]
    outgoing = jnp.dot(send, rows_here, preferred_element_type=F32).astype(BF)
    outgoing = outgoing.reshape(blocks, CAP, width)
    incoming = lax.all_to_all(outgoing, "req", 0, 0).reshape(blocks * CAP, width)
    return jnp.dot(take, incoming, preferred_element_type=F32).astype(BF)


def head_masks(feat_share, head_dim):
    head_count = feat_share // head_dim
    owner = jnp.arange(feat_share, dtype=jnp.int32) // head_dim
    return owner[None, :] == jnp.arange(head_count, dtype=jnp.int32)[:, None]


def spread_query(query_flat, mask):
    return jnp.where(mask[None, :, :], query_flat[:, None, :], jnp.zeros((), query_flat.dtype))


def own_scores(query_flat, key_new, mask, score_scale):
    product = query_flat.astype(jnp.float32) * key_new.astype(jnp.float32)
    return jnp.sum(jnp.where(mask[None, :, :], product[:, None, :], 0.0), axis=-1) * score_scale


def finish_mix(scores, own_score, value_new, mask, mix_fn):
    row_max = jnp.maximum(jnp.max(scores, axis=-1), own_score)
    exp_cache = jnp.exp(scores - row_max[..., None])
    exp_own = jnp.exp(own_score - row_max)
    row_total = jnp.sum(exp_cache, axis=-1) + exp_own
    cache_weights = (exp_cache / row_total[..., None]).astype(jnp.bfloat16)
    own_weight = (exp_own / row_total).astype(jnp.bfloat16).astype(jnp.float32)
    mixed_wide = mix_fn(cache_weights)
    mixed_cache = jnp.sum(jnp.where(mask[None, :, :], mixed_wide, 0.0), axis=1)
    own_spread = jnp.sum(jnp.where(mask[None, :, :], own_weight[:, :, None], 0.0), axis=1)
    return mixed_cache + own_spread * value_new.astype(jnp.float32)


def attend_pool(
    query_flat, key_new, value_new, key_pool, value_pool, local_table, lengths, score_scale, mask
):
    req_rows, feat_share = query_flat.shape
    pool_pages, page_len = (key_pool.shape[0], key_pool.shape[1])
    slot_count = local_table.shape[1]
    page_ids = jnp.arange(pool_pages, dtype=jnp.int32)
    slot_ids = jnp.arange(slot_count, dtype=jnp.int32)
    slot_used = slot_ids[None, :] * page_len < lengths[:, None]
    page_hit = (local_table[:, :, None] == page_ids[None, None, :]) & slot_used[:, :, None]
    start_pos = jnp.sum(jnp.where(page_hit, slot_ids[None, :, None] * page_len, 0), axis=1)
    is_owned = jnp.any(page_hit, axis=1)
    position = start_pos[:, :, None] + jnp.arange(page_len, dtype=jnp.int32)[None, None, :]
    is_valid = (is_owned[:, :, None] & (position < lengths[:, None, None])).reshape(
        req_rows, pool_pages * page_len
    )
    flat_keys = key_pool.reshape(pool_pages * page_len, feat_share)
    flat_values = value_pool.reshape(pool_pages * page_len, feat_share)
    query_wide = spread_query(query_flat, mask)
    scores = (
        jnp.einsum("rhf,tf->rht", query_wide, flat_keys, preferred_element_type=jnp.float32)
        * score_scale
    )
    scores = jnp.where(is_valid[:, None, :], scores, -jnp.inf)
    own_score = own_scores(query_flat, key_new, mask, score_scale)

    def mix_pool(cache_weights):
        return jnp.einsum(
            "rht,tf->rhf", cache_weights, flat_values, preferred_element_type=jnp.float32
        )

    return finish_mix(scores, own_score, value_new, mask, mix_pool)


def local(
    tokens,
    deal_order,
    page_table,
    lengths,
    qkv_weight,
    out_weight,
    up_weight,
    down_weight,
    key_cache,
    value_cache,
    attn_norm,
    mlp_norm,
):
    req_rows, model_width = tokens.shape
    tp_count = lax.axis_size("tp")
    req_index = lax.axis_index("req")
    feat_share = model_width // tp_count
    score_scale = 1.0 / math.sqrt(HD)
    mask = head_masks(feat_share, HD)
    blocks = lax.axis_size("req")
    send, take = deal_maps(deal_order, req_index, req_rows, blocks)
    current = exchange(tokens, send, take, blocks)
    pool_pages = key_cache.shape[1]
    local_table = page_table - req_index * pool_pages
    qkv_flat = qkv_weight.reshape(model_width, 3 * feat_share)
    for layer_index in range(key_cache.shape[0]):
        projected = jnp.dot(current, qkv_flat, preferred_element_type=jnp.float32).astype(
            jnp.bfloat16
        )
        query_flat = projected[:, :feat_share]
        key_new = projected[:, feat_share : 2 * feat_share]
        value_new = projected[:, 2 * feat_share :]
        key_pool = key_cache[layer_index]
        value_pool = value_cache[layer_index]
        attended = attend_pool(
            query_flat,
            key_new,
            value_new,
            key_pool,
            value_pool,
            local_table,
            lengths,
            score_scale,
            mask,
        )
        attended = attended.astype(jnp.bfloat16)
        attn_term = jnp.dot(attended, out_weight, preferred_element_type=jnp.float32)
        hidden = post_norm(attn_term, current, attn_norm)
        up_proj = jnp.dot(hidden, up_weight, preferred_element_type=jnp.float32)
        activated = jax.nn.gelu(up_proj, approximate=True).astype(jnp.bfloat16)
        down_term = jnp.dot(activated, down_weight, preferred_element_type=jnp.float32)
        current = post_norm(down_term, hidden, mlp_norm)
    return exchange(current, take.T, send.T, blocks)


def solution(mesh):
    in_specs = (
        P("req", None),
        P(),
        P("req", None),
        P("req"),
        P(None, None, "tp"),
        P("tp", None),
        P(None, "tp"),
        P("tp", None),
        P(None, "req", None, "tp"),
        P(None, "req", None, "tp"),
        P(),
        P(),
    )
    out_specs = P("req", None)
    return jax.shard_map(local, mesh=mesh, in_specs=in_specs, out_specs=out_specs, check_vma=False)
```

```python
import math

import jax
import jax.numpy as jnp
from jax import lax
from jax.experimental import pallas as pl
from jax.experimental.pallas import tpu as pltpu
from jax.sharding import PartitionSpec as P

HD = 128
CAP = 2
EPS = 1e-6
BF = jnp.bfloat16
F32 = jnp.float32
MIB = 1 << 20
VMEM_SPEC = pl.BlockSpec(memory_space=pltpu.VMEM)
ANY_SPEC = pl.BlockSpec(memory_space=pl.ANY)


def kernel_call(body, out_shape, scratch, limit_mib, *operands):
    return pl.pallas_call(
        body,
        out_shape=out_shape,
        in_specs=[VMEM_SPEC] * len(operands),
        out_specs=jax.tree.map(lambda _: VMEM_SPEC, out_shape),
        scratch_shapes=scratch,
        compiler_params=pltpu.CompilerParams(vmem_limit_bytes=limit_mib * MIB),
    )(*operands)


def on_chip(array):
    return pltpu.with_memory_space_constraint(array, pltpu.VMEM)


def add_norm(parts, residual, gain_bias):
    total = residual.astype(F32)
    for part in parts:
        total = total + part.astype(F32)
    width = total.shape[-1]
    row_mean = jnp.sum(total, axis=-1, keepdims=True) * (1.0 / width)
    centered = total - row_mean
    row_var = jnp.sum(centered * centered, axis=-1, keepdims=True) * (1.0 / width)
    return (centered * lax.rsqrt(row_var + EPS) * gain_bias[0:1, :] + gain_bias[1:2, :]).astype(BF)


def attend(x, wait, w_qkv, k_ref, v_ref, w_out, bias, s_ref, p_ref):
    rows = x.shape[0]
    share = w_qkv.shape[2]
    heads = share // HD
    pages, page_len = k_ref.shape[:2]
    step = k_step(pages)
    span = step * page_len
    scale = 1.0 / math.sqrt(HD)
    projected = []
    for i in range(3):
        wait("qkv", i)
        projected.append(jnp.dot(x, w_qkv[i], preferred_element_type=F32).astype(BF))
    query, fresh_key, fresh_value = projected
    lane_head = lax.broadcasted_iota(jnp.int32, (rows, share), 1) // HD
    wide = jnp.concatenate(
        [jnp.where(lane_head == h, query.astype(F32), 0.0) for h in range(heads)], axis=0
    )
    own_key = jnp.concatenate([fresh_key.astype(F32)] * heads, axis=0)
    own = jnp.sum(wide * own_key, axis=-1, keepdims=True)
    wide = wide.astype(BF)
    peak = jnp.full((heads * rows, HD), -jnp.inf, F32)
    for c in range(pages // step):
        wait("key", c)
        keys = k_ref[c * step : (c + 1) * step].reshape(span, share)
        scores = lax.dot_general(wide, keys, (((1,), (1,)), ((), ())), preferred_element_type=F32)
        here = bias[:, c * span : (c + 1) * span]
        scores = scores + jnp.concatenate([here] * heads, axis=0)
        s_ref[:, c * span : (c + 1) * span] = scores
        for i in range(span // HD):
            peak = jnp.maximum(peak, scores[:, i * HD : (i + 1) * HD])
    peak = jnp.maximum(jnp.max(peak, axis=-1, keepdims=True), own)
    sums = jnp.zeros((heads * rows, HD), F32)
    for c in range(pages // step):
        weight = jnp.exp((s_ref[:, c * span : (c + 1) * span] - peak) * scale)
        p_ref[:, c * span : (c + 1) * span] = weight.astype(BF)
        for i in range(span // HD):
            sums = sums + weight[:, i * HD : (i + 1) * HD]
    own_weight = jnp.exp((own - peak) * scale)
    total = jnp.sum(sums, axis=-1, keepdims=True) + own_weight
    wait("value", 0)
    values = v_ref[...].reshape(pages * page_len, share)
    mixed = jnp.dot(p_ref[...], values, preferred_element_type=F32)
    fresh_value = fresh_value.astype(F32)
    own_weight = own_weight.astype(BF).astype(F32)
    attended = []
    for h in range(heads):
        r = slice(h * rows, (h + 1) * rows)
        f = slice(h * HD, (h + 1) * HD)
        attended.append((mixed[r, f] + own_weight[r] * fresh_value[:, f]) / total[r])
    attended = jnp.concatenate(attended, axis=1).astype(BF)
    wait("out", 0)
    return jnp.dot(attended, w_out[...], preferred_element_type=F32).astype(BF)


def k_step(pages):
    return math.gcd(pages, 6)


def cache_copies(k_hbm, v_hbm, layer, k_ref, v_ref, sems):
    pages = k_ref.shape[0]
    step = k_step(pages)
    copies = {}
    for c in range(pages // step):
        part = pl.ds(c * step, step)
        copies["key", c] = pltpu.make_async_copy(k_hbm.at[layer, part], k_ref.at[part], sems.at[c])
    copies["value", 0] = pltpu.make_async_copy(v_hbm.at[layer], v_ref, sems.at[pages // step])
    return copies


def attention_scratch(rows, key_cache):
    pages, page_len, share = key_cache.shape[1:]
    wide = (rows * share // HD, pages * page_len)
    pool = (pages, page_len, share)
    return [
        pltpu.VMEM(wide, F32),
        pltpu.VMEM(wide, BF),
        pltpu.VMEM(pool, BF),
        pltpu.VMEM(pool, BF),
        pltpu.SemaphoreType.DMA((pages // k_step(pages) + 1,)),
    ]


def first_attention(incoming, take, w_qkv, w_out, key_cache, value_cache, bias):
    rows = bias.shape[0]
    lines, share = incoming.shape
    cols = take.shape[0] // rows

    def body(in_ref, take_ref, b_ref, wq_hbm, wo_hbm, k_hbm, v_hbm, x_ref, out_ref, wq_ref, wo_ref,
             s_ref, p_ref, k_ref, v_ref, sems, w_sems):
        copies = {
            ("qkv", i): pltpu.make_async_copy(wq_hbm.at[i], wq_ref.at[i], w_sems.at[i]) for i in range(3)
        }
        copies.update(cache_copies(k_hbm, v_hbm, 0, k_ref, v_ref, sems))
        copies["out", 0] = pltpu.make_async_copy(wo_hbm, wo_ref, w_sems.at[3])
        for copy in copies.values():
            copy.start()
        stacked = jnp.dot(take_ref[...], in_ref[...], preferred_element_type=F32).astype(BF)
        x = jnp.concatenate([stacked[c * rows : (c + 1) * rows] for c in range(cols)], axis=1)
        x_ref[...] = x
        out_ref[...] = attend(
            x, lambda *key: copies[key].wait(), wq_ref, k_ref, v_ref, wo_ref, b_ref, s_ref, p_ref
        )

    shape = jax.ShapeDtypeStruct((rows, share * cols), BF)
    return pl.pallas_call(
        body,
        out_shape=(shape, shape, pltpu.VMEM(w_qkv.shape, BF), pltpu.VMEM(w_out.shape, BF)),
        in_specs=[VMEM_SPEC] * 3 + [ANY_SPEC] * 4,
        out_specs=(VMEM_SPEC,) * 4,
        scratch_shapes=attention_scratch(rows, key_cache) + [pltpu.SemaphoreType.DMA((4,))],
        compiler_params=pltpu.CompilerParams(vmem_limit_bytes=20 * MIB),
    )(incoming, take, bias, w_qkv, w_out, key_cache, value_cache)


def norm_attention(parts, residual, gain_bias, w_qkv, w_out, key_cache, value_cache, bias, layer):
    count = len(parts)

    def body(*refs):
        part_refs, (res_ref, norm_ref, wq_ref, wo_ref, b_ref, k_hbm, v_hbm) = refs[:count], refs[count : count + 7]
        x_ref, out_ref, s_ref, p_ref, k_ref, v_ref, sems = refs[count + 7 :]
        copies = cache_copies(k_hbm, v_hbm, layer, k_ref, v_ref, sems)
        for copy in copies.values():
            copy.start()
        x = add_norm([r[...] for r in part_refs], res_ref[...], norm_ref[...])
        x_ref[...] = x

        def wait(*key):
            if key in copies:
                copies[key].wait()

        out_ref[...] = attend(x, wait, wq_ref, k_ref, v_ref, wo_ref, b_ref, s_ref, p_ref)

    shape = jax.ShapeDtypeStruct(residual.shape, BF)
    return pl.pallas_call(
        body,
        out_shape=(shape, shape),
        in_specs=[VMEM_SPEC] * (count + 5) + [ANY_SPEC] * 2,
        out_specs=(VMEM_SPEC, VMEM_SPEC),
        scratch_shapes=attention_scratch(residual.shape[0], key_cache),
        compiler_params=pltpu.CompilerParams(vmem_limit_bytes=20 * MIB),
    )(*parts, residual, gain_bias, w_qkv, w_out, bias, key_cache, value_cache)


def norm_mlp(parts, residual, gain_bias, w_up, w_down):
    count = len(parts)

    def body(*refs):
        part_refs, (res_ref, norm_ref, up_ref, down_ref) = refs[:count], refs[count : count + 4]
        x_ref, out_ref = refs[count + 4 :]
        x = add_norm([r[...] for r in part_refs], res_ref[...], norm_ref[...])
        x_ref[...] = x
        up = jnp.dot(x, up_ref[...], preferred_element_type=F32)
        active = jax.nn.gelu(up, approximate=True).astype(BF)
        out_ref[...] = jnp.dot(active, down_ref[...], preferred_element_type=F32).astype(BF)

    shape = jax.ShapeDtypeStruct(residual.shape, BF)
    return kernel_call(body, (shape, shape), [], 8, *parts, residual, gain_bias, w_up, w_down)


def norm_send(parts, residual, gain_bias, give):
    count = len(parts)
    cols = give.shape[1] // residual.shape[0]
    share = residual.shape[1] // cols

    def body(*refs):
        res_ref, norm_ref, give_ref, out_ref = refs[count:]
        x = add_norm([r[...] for r in refs[:count]], res_ref[...], norm_ref[...])
        out_ref[...] = lay_out(give_ref[...], x, cols)

    shape = jax.ShapeDtypeStruct((give.shape[0], share), BF)
    return kernel_call(body, shape, [], 8, *parts, residual, gain_bias, give)


def lay_out(give, rows_here, cols):
    share = rows_here.shape[1] // cols
    stacked = jnp.concatenate([rows_here[:, c * share : (c + 1) * share] for c in range(cols)], axis=0)
    return jnp.dot(give, stacked, preferred_element_type=F32).astype(BF)


def gather_parts(part):
    size = lax.axis_size("tp")
    return [part] + [
        lax.ppermute(part, "tp", [(i, (i + step) % size) for i in range(size)])
        for step in range(1, size)
    ]


def iota(shape, dim):
    return lax.broadcasted_iota(jnp.int32, shape, dim)


def deal_send(order, tokens, blocks, cols):
    rows, width = tokens.shape
    lines, stack = blocks * CAP * cols, cols * rows

    def body(order_ref, tok_ref, out_ref, give_ref):
        first = lax.axis_index("req") * rows
        wanted = first + iota((stack, order.shape[1]), 0) % rows
        goes = jnp.concatenate(
            [(order_ref[r : r + 1, :] == wanted).astype(F32).astype(BF) for r in range(order.shape[0])], axis=1
        )
        slots = order.shape[0] * order.shape[1]
        block_of = (iota((blocks, slots), 1) // rows == iota((blocks, slots), 0)).astype(F32).astype(BF)
        sent = lax.dot_general(block_of, goes, (((1,), (1,)), ((), ())), preferred_element_type=F32)
        a, b = iota((stack, stack), 0), iota((stack, stack), 1)
        earlier = ((a // rows == b // rows) & (a < b)).astype(F32).astype(BF)
        rank = jnp.dot(sent.astype(BF), earlier, preferred_element_type=F32)
        line, block = iota((lines, blocks), 0), iota((lines, blocks), 1)
        give = jnp.zeros((lines, stack), F32)
        for k in range(CAP):
            spread = (line // cols == block * CAP + k).astype(F32).astype(BF)
            chosen = jnp.where(rank == k, sent, 0.0).astype(BF)
            give = give + jnp.dot(spread, chosen, preferred_element_type=F32)
        same = iota((lines, stack), 0) % cols == iota((lines, stack), 1) // rows
        give = jnp.where(same, give, 0.0)
        give_ref[...] = give
        out_ref[...] = lay_out(give.astype(BF), tok_ref[...], cols)

    out = (jax.ShapeDtypeStruct((lines, width // cols), BF), jax.ShapeDtypeStruct((lines, stack), F32))
    return kernel_call(body, out, [], 8, order, tokens)


def deal_take(order, give, table, lengths, cols, pages, page_len):
    rows = lengths.shape[1]
    lines, stack = give.shape

    def body(order_ref, give_ref, table_ref, len_ref, take_ref, back_ref, send_ref, bias_ref):
        req = lax.axis_index("req")
        slot = req * rows + iota((stack, order.shape[1]), 0) % rows
        mine = jnp.zeros((stack, order.shape[1]), F32)
        for r in range(order.shape[0]):
            here = iota((stack, order.shape[1]), 1) + r * order.shape[1]
            mine = mine + jnp.where(here == slot, order_ref[r : r + 1, :], 0).astype(F32)
        column = jnp.broadcast_to(jnp.sum(mine, axis=1, keepdims=True), (stack, stack))
        line_of = jnp.transpose(column).astype(jnp.int32)
        column = column.astype(jnp.int32)
        a, b = iota((stack, stack), 0), iota((stack, stack), 1)
        before = (b < rows) & (column // rows == line_of // rows) & (line_of < column)
        rank = jnp.sum(before.astype(F32), axis=1, keepdims=True).astype(jnp.int32)
        place = (column[:, 0:1] // rows * CAP + rank) * cols + iota((stack, 1), 0) // rows
        take = (iota((stack, lines), 1) == place).astype(F32)
        take_ref[...] = take.astype(BF)
        send_ref[...] = jnp.transpose(take).astype(BF)
        back_ref[...] = jnp.transpose(give_ref[...]).astype(BF)
        diagonal = iota((rows, rows), 0) == iota((rows, rows), 1)

        def stand(line):
            return jnp.sum(jnp.where(diagonal, line, 0).astype(F32), axis=1, keepdims=True).astype(jnp.int32)

        length = stand(len_ref[...])
        page = iota((rows, page_len), 1) + req * pages
        room = jnp.zeros((rows, page_len), jnp.int32)
        for k in range(table.shape[0]):
            left = length - k * page_len
            hit = (stand(table_ref[k : k + 1, :]) == page) & (left > 0)
            room = room + jnp.where(hit, left, 0)
        offset = iota((rows, page_len), 1)
        for p in range(pages):
            bias_ref[:, p * page_len : (p + 1) * page_len] = jnp.where(
                offset < room[:, p : p + 1], 0.0, -jnp.inf
            ).astype(F32)

    out = (
        jax.ShapeDtypeStruct((stack, lines), BF),
        jax.ShapeDtypeStruct((stack, lines), BF),
        jax.ShapeDtypeStruct((lines, stack), BF),
        jax.ShapeDtypeStruct((rows, pages * page_len), F32),
    )
    return kernel_call(body, out, [], 8, order, give, table, lengths)


def settle(incoming, back, rows):
    cols = back.shape[0] // rows

    def body(in_ref, back_ref, out_ref):
        stacked = jnp.dot(back_ref[...], in_ref[...], preferred_element_type=F32).astype(BF)
        out_ref[...] = jnp.concatenate([stacked[c * rows : (c + 1) * rows] for c in range(cols)], axis=1)

    shape = jax.ShapeDtypeStruct((rows, incoming.shape[1] * cols), BF)
    return kernel_call(body, shape, [], 8, incoming, back)


def swap(lines_out, blocks):
    lines, share = lines_out.shape
    return lax.all_to_all(lines_out.reshape(blocks, lines // blocks, share), "req", 0, 0).reshape(lines, share)


def local(
    tokens,
    deal_order,
    page_table,
    lengths,
    qkv_weight,
    out_weight,
    up_weight,
    down_weight,
    key_cache,
    value_cache,
    attn_norm,
    mlp_norm,
):
    req_rows = tokens.shape[0]
    blocks = lax.axis_size("req")
    cols = lax.axis_size("tp")
    layers, pool_pages, page_len = key_cache.shape[:3]
    order = deal_order.reshape(-1, HD)
    outgoing, give = deal_send(order, tokens, blocks, cols)
    incoming = swap(outgoing, blocks)
    take, back, send, bias = deal_take(
        order, give, page_table.T, lengths.reshape(1, -1), cols, pool_pages, page_len
    )
    w_qkv = jnp.transpose(qkv_weight, (1, 0, 2))
    w_up = on_chip(up_weight)
    w_down = on_chip(down_weight)
    current, partial, w_qkv, w_out = first_attention(
        incoming, take, w_qkv, out_weight, key_cache, value_cache, bias
    )
    for layer in range(layers):
        hidden, partial = norm_mlp(gather_parts(partial), current, attn_norm, w_up, w_down)
        if layer + 1 < layers:
            current, partial = norm_attention(
                gather_parts(partial), hidden, mlp_norm, w_qkv, w_out, key_cache, value_cache, bias, layer + 1
            )
    leaving = norm_send(gather_parts(partial), hidden, mlp_norm, send)
    return settle(swap(leaving, blocks), back, req_rows)


def solution(mesh):
    in_specs = (
        P("req", None),
        P(),
        P("req", None),
        P("req"),
        P(None, None, "tp"),
        P("tp", None),
        P(None, "tp"),
        P("tp", None),
        P(None, "req", None, "tp"),
        P(None, "req", None, "tp"),
        P(),
        P(),
    )
    out_specs = P("req", None)
    return jax.shard_map(local, mesh=mesh, in_specs=in_specs, out_specs=out_specs, check_vma=False)
```

```python
import math

import jax
import jax.numpy as jnp
from jax import lax
from jax.experimental import pallas as pl
from jax.experimental.pallas import tpu as pltpu
from jax.sharding import PartitionSpec as P

HD = 128
CAP = 2
EPS = 1e-6
BF = jnp.bfloat16
F32 = jnp.float32
MIB = 1 << 20
VMEM_SPEC = pl.BlockSpec(memory_space=pltpu.VMEM)
HBM_SPEC = pl.BlockSpec(memory_space=pltpu.HBM)


def kernel_call(body, out_shape, scratch, limit_mib, *operands):
    return pl.pallas_call(
        body,
        out_shape=out_shape,
        in_specs=[VMEM_SPEC] * len(operands),
        out_specs=jax.tree.map(lambda _: VMEM_SPEC, out_shape),
        scratch_shapes=scratch,
        compiler_params=pltpu.CompilerParams(vmem_limit_bytes=limit_mib * MIB),
    )(*operands)


def in_place(array):
    return pltpu.with_memory_space_constraint(array, pltpu.HBM)


def on_chip(array):
    return pltpu.with_memory_space_constraint(array, pltpu.VMEM)


def add_norm(parts, residual, gain_bias):
    total = residual.astype(F32)
    for part in parts:
        total = total + part.astype(F32)
    width = total.shape[-1]
    row_mean = jnp.sum(total, axis=-1, keepdims=True) * (1.0 / width)
    centered = total - row_mean
    row_var = jnp.sum(centered * centered, axis=-1, keepdims=True) * (1.0 / width)
    return (centered * lax.rsqrt(row_var + EPS) * gain_bias[0:1, :] + gain_bias[1:2, :]).astype(BF)


def attend(x, wait, w_qkv, k_ref, v_ref, w_out, bias, s_ref, p_ref):
    rows = x.shape[0]
    share = w_qkv.shape[2]
    heads = share // HD
    pages, page_len = k_ref.shape[:2]
    step = k_step(pages)
    span = step * page_len
    scale = 1.0 / math.sqrt(HD)
    projected = []
    for i in range(3):
        wait("qkv", i)
        projected.append(jnp.dot(x, w_qkv[i], preferred_element_type=F32).astype(BF))
    query, fresh_key, fresh_value = projected
    lane_head = lax.broadcasted_iota(jnp.int32, (rows, share), 1) // HD
    wide = jnp.concatenate(
        [jnp.where(lane_head == h, query.astype(F32), 0.0) for h in range(heads)], axis=0
    )
    own_key = jnp.concatenate([fresh_key.astype(F32)] * heads, axis=0)
    own = jnp.sum(wide * own_key, axis=-1, keepdims=True)
    wide = wide.astype(BF)
    peak = jnp.full((heads * rows, HD), -jnp.inf, F32)
    for c in range(pages // step):
        wait("key", c)
        keys = k_ref[c * step : (c + 1) * step].reshape(span, share)
        scores = lax.dot_general(wide, keys, (((1,), (1,)), ((), ())), preferred_element_type=F32)
        here = bias[:, c * span : (c + 1) * span]
        scores = scores + jnp.concatenate([here] * heads, axis=0)
        s_ref[:, c * span : (c + 1) * span] = scores
        for i in range(span // HD):
            peak = jnp.maximum(peak, scores[:, i * HD : (i + 1) * HD])
    peak = jnp.maximum(jnp.max(peak, axis=-1, keepdims=True), own)
    sums = jnp.zeros((heads * rows, HD), F32)
    for c in range(pages // step):
        weight = jnp.exp((s_ref[:, c * span : (c + 1) * span] - peak) * scale)
        p_ref[:, c * span : (c + 1) * span] = weight.astype(BF)
        for i in range(span // HD):
            sums = sums + weight[:, i * HD : (i + 1) * HD]
    own_weight = jnp.exp((own - peak) * scale)
    total = jnp.sum(sums, axis=-1, keepdims=True) + own_weight
    wait("value", 0)
    values = v_ref[...].reshape(pages * page_len, share)
    mixed = jnp.dot(p_ref[...], values, preferred_element_type=F32)
    fresh_value = fresh_value.astype(F32)
    own_weight = own_weight.astype(BF).astype(F32)
    attended = []
    for h in range(heads):
        r = slice(h * rows, (h + 1) * rows)
        f = slice(h * HD, (h + 1) * HD)
        attended.append((mixed[r, f] + own_weight[r] * fresh_value[:, f]) / total[r])
    attended = jnp.concatenate(attended, axis=1).astype(BF)
    wait("out", 0)
    return jnp.dot(attended, w_out[...], preferred_element_type=F32).astype(BF)


def k_step(pages):
    return math.gcd(pages, 6)


def cache_copies(k_hbm, v_hbm, layer, k_ref, v_ref, sems):
    pages = k_ref.shape[0]
    step = k_step(pages)
    copies = {}
    for c in range(pages // step):
        part = pl.ds(c * step, step)
        copies["key", c] = pltpu.make_async_copy(k_hbm.at[layer, part], k_ref.at[part], sems.at[c])
    copies["value", 0] = pltpu.make_async_copy(v_hbm.at[layer], v_ref, sems.at[pages // step])
    return copies


def attention_scratch(rows, key_cache):
    pages, page_len, share = key_cache.shape[1:]
    wide = (rows * share // HD, pages * page_len)
    pool = (pages, page_len, share)
    return [
        pltpu.VMEM(wide, F32),
        pltpu.VMEM(wide, BF),
        pltpu.VMEM(pool, BF),
        pltpu.VMEM(pool, BF),
        pltpu.SemaphoreType.DMA((pages // k_step(pages) + 1,)),
    ]


def first_attention(incoming, take, w_qkv, w_out, key_cache, value_cache, bias):
    rows = bias.shape[0]
    lines, share = incoming.shape
    cols = take.shape[0] // rows

    def body(in_ref, take_ref, b_ref, wq_hbm, wo_hbm, k_hbm, v_hbm, x_ref, out_ref, wq_ref, wo_ref,
             s_ref, p_ref, k_ref, v_ref, sems, w_sems):
        copies = {
            ("qkv", i): pltpu.make_async_copy(wq_hbm.at[i], wq_ref.at[i], w_sems.at[i]) for i in range(3)
        }
        copies.update(cache_copies(k_hbm, v_hbm, 0, k_ref, v_ref, sems))
        copies["out", 0] = pltpu.make_async_copy(wo_hbm, wo_ref, w_sems.at[3])
        for copy in copies.values():
            copy.start()
        stacked = jnp.dot(take_ref[...], in_ref[...], preferred_element_type=F32).astype(BF)
        x = jnp.concatenate([stacked[c * rows : (c + 1) * rows] for c in range(cols)], axis=1)
        x_ref[...] = x
        out_ref[...] = attend(
            x, lambda *key: copies[key].wait(), wq_ref, k_ref, v_ref, wo_ref, b_ref, s_ref, p_ref
        )

    shape = jax.ShapeDtypeStruct((rows, share * cols), BF)
    return pl.pallas_call(
        body,
        out_shape=(shape, shape, pltpu.VMEM(w_qkv.shape, BF), pltpu.VMEM(w_out.shape, BF)),
        in_specs=[VMEM_SPEC] * 3 + [HBM_SPEC] * 4,
        out_specs=(VMEM_SPEC,) * 4,
        scratch_shapes=attention_scratch(rows, key_cache) + [pltpu.SemaphoreType.DMA((4,))],
        compiler_params=pltpu.CompilerParams(vmem_limit_bytes=20 * MIB),
    )(incoming, take, bias, *map(in_place, (w_qkv, w_out, key_cache, value_cache)))


def norm_attention(parts, residual, gain_bias, w_qkv, w_out, key_cache, value_cache, bias, layer):
    count = len(parts)

    def body(*refs):
        part_refs, (res_ref, norm_ref, wq_ref, wo_ref, b_ref, k_hbm, v_hbm) = refs[:count], refs[count : count + 7]
        x_ref, out_ref, s_ref, p_ref, k_ref, v_ref, sems = refs[count + 7 :]
        copies = cache_copies(k_hbm, v_hbm, layer, k_ref, v_ref, sems)
        for copy in copies.values():
            copy.start()
        x = add_norm([r[...] for r in part_refs], res_ref[...], norm_ref[...])
        x_ref[...] = x

        def wait(*key):
            if key in copies:
                copies[key].wait()

        out_ref[...] = attend(x, wait, wq_ref, k_ref, v_ref, wo_ref, b_ref, s_ref, p_ref)

    shape = jax.ShapeDtypeStruct(residual.shape, BF)
    return pl.pallas_call(
        body,
        out_shape=(shape, shape),
        in_specs=[VMEM_SPEC] * (count + 5) + [HBM_SPEC] * 2,
        out_specs=(VMEM_SPEC, VMEM_SPEC),
        scratch_shapes=attention_scratch(residual.shape[0], key_cache),
        compiler_params=pltpu.CompilerParams(vmem_limit_bytes=20 * MIB),
    )(*parts, residual, gain_bias, w_qkv, w_out, bias, in_place(key_cache), in_place(value_cache))


def norm_mlp(parts, residual, gain_bias, w_up, w_down):
    count = len(parts)

    def body(*refs):
        part_refs, (res_ref, norm_ref, up_ref, down_ref) = refs[:count], refs[count : count + 4]
        x_ref, out_ref = refs[count + 4 :]
        x = add_norm([r[...] for r in part_refs], res_ref[...], norm_ref[...])
        x_ref[...] = x
        up = jnp.dot(x, up_ref[...], preferred_element_type=F32)
        active = jax.nn.gelu(up, approximate=True).astype(BF)
        out_ref[...] = jnp.dot(active, down_ref[...], preferred_element_type=F32).astype(BF)

    shape = jax.ShapeDtypeStruct(residual.shape, BF)
    return kernel_call(body, (shape, shape), [], 8, *parts, residual, gain_bias, w_up, w_down)


def norm_send(parts, residual, gain_bias, give):
    count = len(parts)
    cols = give.shape[1] // residual.shape[0]
    share = residual.shape[1] // cols

    def body(*refs):
        res_ref, norm_ref, give_ref, out_ref = refs[count:]
        x = add_norm([r[...] for r in refs[:count]], res_ref[...], norm_ref[...])
        out_ref[...] = lay_out(give_ref[...], x, cols)

    shape = jax.ShapeDtypeStruct((give.shape[0], share), BF)
    return kernel_call(body, shape, [], 8, *parts, residual, gain_bias, give)


def lay_out(give, rows_here, cols):
    share = rows_here.shape[1] // cols
    stacked = jnp.concatenate([rows_here[:, c * share : (c + 1) * share] for c in range(cols)], axis=0)
    return jnp.dot(give, stacked, preferred_element_type=F32).astype(BF)


def gather_parts(part):
    size = lax.axis_size("tp")
    return [part] + [
        lax.ppermute(part, "tp", [(i, (i + step) % size) for i in range(size)])
        for step in range(1, size)
    ]


def iota(shape, dim):
    return lax.broadcasted_iota(jnp.int32, shape, dim)


def deal_send(order, tokens, blocks, cols):
    rows, width = tokens.shape
    lines, stack = blocks * CAP * cols, cols * rows

    def body(order_hbm, tok_hbm, out_ref, give_ref, order_ref, tok_ref, sems):
        order_copy = pltpu.make_async_copy(order_hbm, order_ref, sems.at[0])
        token_copy = pltpu.make_async_copy(tok_hbm, tok_ref, sems.at[1])
        order_copy.start()
        token_copy.start()
        first = lax.axis_index("req") * rows
        order_copy.wait()
        wanted = first + iota((stack, order.shape[1]), 0) % rows
        goes = jnp.concatenate(
            [(order_ref[r : r + 1, :] == wanted).astype(F32).astype(BF) for r in range(order.shape[0])], axis=1
        )
        slots = order.shape[0] * order.shape[1]
        block_of = (iota((blocks, slots), 1) // rows == iota((blocks, slots), 0)).astype(F32).astype(BF)
        sent = lax.dot_general(block_of, goes, (((1,), (1,)), ((), ())), preferred_element_type=F32)
        a, b = iota((stack, stack), 0), iota((stack, stack), 1)
        earlier = ((a // rows == b // rows) & (a < b)).astype(F32).astype(BF)
        rank = jnp.dot(sent.astype(BF), earlier, preferred_element_type=F32)
        line, block = iota((lines, blocks), 0), iota((lines, blocks), 1)
        give = jnp.zeros((lines, stack), F32)
        for k in range(CAP):
            spread = (line // cols == block * CAP + k).astype(F32).astype(BF)
            chosen = jnp.where(rank == k, sent, 0.0).astype(BF)
            give = give + jnp.dot(spread, chosen, preferred_element_type=F32)
        same = iota((lines, stack), 0) % cols == iota((lines, stack), 1) // rows
        give = jnp.where(same, give, 0.0)
        give_ref[...] = give
        token_copy.wait()
        out_ref[...] = lay_out(give.astype(BF), tok_ref[...], cols)

    return pl.pallas_call(
        body,
        out_shape=(jax.ShapeDtypeStruct((lines, width // cols), BF), jax.ShapeDtypeStruct((lines, stack), F32)),
        in_specs=[HBM_SPEC] * 2,
        out_specs=(VMEM_SPEC,) * 2,
        scratch_shapes=[
            pltpu.VMEM(order.shape, order.dtype),
            pltpu.VMEM(tokens.shape, BF),
            pltpu.SemaphoreType.DMA((2,)),
        ],
        compiler_params=pltpu.CompilerParams(vmem_limit_bytes=8 * MIB),
    )(in_place(order), in_place(tokens))


def deal_take(order, give, table, lengths, cols, pages, page_len):
    rows = lengths.shape[1]
    lines, stack = give.shape

    def body(order_ref, give_ref, table_ref, len_ref, take_ref, back_ref, send_ref, bias_ref):
        req = lax.axis_index("req")
        slot = req * rows + iota((stack, order.shape[1]), 0) % rows
        mine = jnp.zeros((stack, order.shape[1]), F32)
        for r in range(order.shape[0]):
            here = iota((stack, order.shape[1]), 1) + r * order.shape[1]
            mine = mine + jnp.where(here == slot, order_ref[r : r + 1, :], 0).astype(F32)
        column = jnp.broadcast_to(jnp.sum(mine, axis=1, keepdims=True), (stack, stack))
        line_of = jnp.transpose(column).astype(jnp.int32)
        column = column.astype(jnp.int32)
        a, b = iota((stack, stack), 0), iota((stack, stack), 1)
        before = (b < rows) & (column // rows == line_of // rows) & (line_of < column)
        rank = jnp.sum(before.astype(F32), axis=1, keepdims=True).astype(jnp.int32)
        place = (column[:, 0:1] // rows * CAP + rank) * cols + iota((stack, 1), 0) // rows
        take = (iota((stack, lines), 1) == place).astype(F32)
        take_ref[...] = take.astype(BF)
        send_ref[...] = jnp.transpose(take).astype(BF)
        back_ref[...] = jnp.transpose(give_ref[...]).astype(BF)
        diagonal = iota((rows, rows), 0) == iota((rows, rows), 1)

        def stand(line):
            return jnp.sum(jnp.where(diagonal, line, 0).astype(F32), axis=1, keepdims=True).astype(jnp.int32)

        length = stand(len_ref[...])
        page = iota((rows, page_len), 1) + req * pages
        room = jnp.zeros((rows, page_len), jnp.int32)
        for k in range(table.shape[0]):
            left = length - k * page_len
            hit = (stand(table_ref[k : k + 1, :]) == page) & (left > 0)
            room = room + jnp.where(hit, left, 0)
        offset = iota((rows, page_len), 1)
        for p in range(pages):
            bias_ref[:, p * page_len : (p + 1) * page_len] = jnp.where(
                offset < room[:, p : p + 1], 0.0, -jnp.inf
            ).astype(F32)

    out = (
        jax.ShapeDtypeStruct((stack, lines), BF),
        jax.ShapeDtypeStruct((stack, lines), BF),
        jax.ShapeDtypeStruct((lines, stack), BF),
        jax.ShapeDtypeStruct((rows, pages * page_len), F32),
    )
    return kernel_call(body, out, [], 8, order, give, table, lengths)


def settle(incoming, back, rows):
    cols = back.shape[0] // rows

    def body(in_ref, back_ref, out_ref):
        stacked = jnp.dot(back_ref[...], in_ref[...], preferred_element_type=F32).astype(BF)
        out_ref[...] = jnp.concatenate([stacked[c * rows : (c + 1) * rows] for c in range(cols)], axis=1)

    shape = jax.ShapeDtypeStruct((rows, incoming.shape[1] * cols), BF)
    return kernel_call(body, shape, [], 8, incoming, back)


def swap(lines_out, blocks):
    lines, share = lines_out.shape
    return lax.all_to_all(lines_out.reshape(blocks, lines // blocks, share), "req", 0, 0).reshape(lines, share)


def local(
    tokens,
    deal_order,
    page_table,
    lengths,
    qkv_weight,
    out_weight,
    up_weight,
    down_weight,
    key_cache,
    value_cache,
    attn_norm,
    mlp_norm,
):
    req_rows = tokens.shape[0]
    blocks = lax.axis_size("req")
    cols = lax.axis_size("tp")
    layers, pool_pages, page_len = key_cache.shape[:3]
    order = deal_order.reshape(-1, HD)
    outgoing, give = deal_send(order, tokens, blocks, cols)
    incoming = swap(outgoing, blocks)
    take, back, send, bias = deal_take(
        order, give, page_table.T, lengths.reshape(1, -1), cols, pool_pages, page_len
    )
    w_qkv = jnp.transpose(qkv_weight, (1, 0, 2))
    w_up = on_chip(up_weight)
    w_down = on_chip(down_weight)
    current, partial, w_qkv, w_out = first_attention(
        incoming, take, w_qkv, out_weight, key_cache, value_cache, bias
    )
    for layer in range(layers):
        hidden, partial = norm_mlp(gather_parts(partial), current, attn_norm, w_up, w_down)
        if layer + 1 < layers:
            current, partial = norm_attention(
                gather_parts(partial), hidden, mlp_norm, w_qkv, w_out, key_cache, value_cache, bias, layer + 1
            )
    leaving = norm_send(gather_parts(partial), hidden, mlp_norm, send)
    return settle(swap(leaving, blocks), back, req_rows)


def solution(mesh):
    in_specs = (
        P("req", None),
        P(),
        P("req", None),
        P("req"),
        P(None, None, "tp"),
        P("tp", None),
        P(None, "tp"),
        P("tp", None),
        P(None, "req", None, "tp"),
        P(None, "req", None, "tp"),
        P(),
        P(),
    )
    out_specs = P("req", None)
    return jax.shard_map(local, mesh=mesh, in_specs=in_specs, out_specs=out_specs, check_vma=False)
```

```python
import math

import jax
import jax.numpy as jnp
from jax import lax
from jax.experimental import pallas as pl
from jax.experimental.pallas import tpu as pltpu
from jax.sharding import PartitionSpec as P

HD = 128
CAP = 2
EPS = 1e-6
BF = jnp.bfloat16
F32 = jnp.float32
MIB = 1 << 20
VMEM_SPEC = pl.BlockSpec(memory_space=pltpu.VMEM)
HBM_SPEC = pl.BlockSpec(memory_space=pltpu.HBM)


def kernel_call(body, out_shape, scratch, limit_mib, *operands):
    return pl.pallas_call(
        body,
        out_shape=out_shape,
        in_specs=[VMEM_SPEC] * len(operands),
        out_specs=jax.tree.map(lambda _: VMEM_SPEC, out_shape),
        scratch_shapes=scratch,
        compiler_params=pltpu.CompilerParams(vmem_limit_bytes=limit_mib * MIB),
    )(*operands)


def in_place(array):
    return pltpu.with_memory_space_constraint(array, pltpu.HBM)


def add_norm(parts, residual, gain_bias):
    total = residual.astype(F32)
    for part in parts:
        total = total + part.astype(F32)
    width = total.shape[-1]
    row_mean = jnp.sum(total, axis=-1, keepdims=True) * (1.0 / width)
    centered = total - row_mean
    row_var = jnp.sum(centered * centered, axis=-1, keepdims=True) * (1.0 / width)
    return (centered * lax.rsqrt(row_var + EPS) * gain_bias[0:1, :] + gain_bias[1:2, :]).astype(BF)


def attend(x, wait, w_qkv, k_ref, v_ref, w_out, bias, s_ref):
    rows = x.shape[0]
    share = w_qkv.shape[2]
    heads = share // HD
    pages, page_len = k_ref.shape[:2]
    step = k_step(pages)
    span = step * page_len
    scale = 1.0 / math.sqrt(HD)
    projected = []
    for i in range(3):
        wait("qkv", i)
        projected.append(jnp.dot(x, w_qkv[i], preferred_element_type=F32).astype(BF))
    query, fresh_key, fresh_value = projected
    lane_head = lax.broadcasted_iota(jnp.int32, (rows, share), 1) // HD
    wide = jnp.concatenate(
        [jnp.where(lane_head == h, query.astype(F32), 0.0) for h in range(heads)], axis=0
    )
    own_key = jnp.concatenate([fresh_key.astype(F32)] * heads, axis=0)
    own = jnp.sum(wide * own_key, axis=-1, keepdims=True)
    wide = wide.astype(BF)
    peak = jnp.full((heads * rows, HD), -jnp.inf, F32)
    for c in range(pages // step):
        wait("key", c)
        keys = k_ref[c * step : (c + 1) * step].reshape(span, share)
        scores = lax.dot_general(wide, keys, (((1,), (1,)), ((), ())), preferred_element_type=F32)
        here = bias[:, c * span : (c + 1) * span]
        scores = scores + jnp.concatenate([here] * heads, axis=0)
        s_ref[:, c * span : (c + 1) * span] = scores
        for i in range(span // HD):
            peak = jnp.maximum(peak, scores[:, i * HD : (i + 1) * HD])
    peak = jnp.maximum(jnp.max(peak, axis=-1, keepdims=True), own)
    sums = jnp.zeros((heads * rows, HD), F32)
    mixed = jnp.zeros((heads * rows, share), F32)
    for c in range(pages // step):
        weight = jnp.exp((s_ref[:, c * span : (c + 1) * span] - peak) * scale)
        for i in range(span // HD):
            sums = sums + weight[:, i * HD : (i + 1) * HD]
        wait("value", c)
        values = v_ref[c * step : (c + 1) * step].reshape(span, share)
        mixed = mixed + jnp.dot(weight.astype(BF), values, preferred_element_type=F32)
    own_weight = jnp.exp((own - peak) * scale)
    total = jnp.sum(sums, axis=-1, keepdims=True) + own_weight
    fresh_value = fresh_value.astype(F32)
    own_weight = own_weight.astype(BF).astype(F32)
    attended = []
    for h in range(heads):
        r = slice(h * rows, (h + 1) * rows)
        f = slice(h * HD, (h + 1) * HD)
        attended.append((mixed[r, f] + own_weight[r] * fresh_value[:, f]) / total[r])
    attended = jnp.concatenate(attended, axis=1).astype(BF)
    wait("out", 0)
    return jnp.dot(attended, w_out[...], preferred_element_type=F32).astype(BF)


def k_step(pages):
    return math.gcd(pages, 6)


def score_scratch(rows, pages, page_len, share):
    return pltpu.VMEM((rows * share // HD, pages * page_len), F32)


def load(after, *sources):
    def body(*refs):
        count = len(sources)
        copies = [
            pltpu.make_async_copy(
                refs[1 + i] if layer is None else refs[1 + i].at[layer], refs[1 + count + i], refs[-1].at[i]
            )
            for i, (_, layer) in enumerate(sources)
        ]
        for copy in copies:
            copy.start()
        for copy in copies:
            copy.wait()

    shapes = [a.shape if layer is None else a.shape[1:] for a, layer in sources]
    size = sum(2 * math.prod(shape) for shape in shapes)
    return pl.pallas_call(
        body,
        out_shape=tuple(pltpu.VMEM(shape, BF) for shape in shapes),
        in_specs=[HBM_SPEC] * (1 + len(sources)),
        out_specs=(VMEM_SPEC,) * len(sources),
        scratch_shapes=[pltpu.SemaphoreType.DMA((len(sources),))],
        compiler_params=pltpu.CompilerParams(vmem_limit_bytes=MIB),
        cost_estimate=pl.CostEstimate(flops=0, transcendentals=0, bytes_accessed=2 * size),
    )(after, *(in_place(a) for a, _ in sources))


def first_attention(incoming, take, w_qkv, w_out, key_cache, value_cache, bias):
    rows = bias.shape[0]
    lines, share = incoming.shape
    cols = take.shape[0] // rows

    pages, page_len = key_cache.shape[1:3]
    step = k_step(pages)
    parts = pages // step

    def body(in_ref, take_ref, b_ref, wq_hbm, wo_hbm, k_hbm, v_hbm, x_ref, out_ref, wq_ref, wo_ref,
             s_ref, k_ref, v_ref, k_sems, v_sems, w_sems):
        copies = {}
        for i in range(3):
            copies["qkv", i] = pltpu.make_async_copy(wq_hbm.at[i], wq_ref.at[i], w_sems.at[i])
        for name, hbm, ref, sems in (("key", k_hbm, k_ref, k_sems), ("value", v_hbm, v_ref, v_sems)):
            for c in range(parts):
                span = pl.ds(c * step, step)
                copies[name, c] = pltpu.make_async_copy(hbm.at[0, span], ref.at[span], sems.at[c])
        copies["out", 0] = pltpu.make_async_copy(wo_hbm, wo_ref, w_sems.at[3])
        for copy in copies.values():
            copy.start()
        stacked = jnp.dot(take_ref[...], in_ref[...], preferred_element_type=F32).astype(BF)
        x = jnp.concatenate([stacked[c * rows : (c + 1) * rows] for c in range(cols)], axis=1)
        x_ref[...] = x
        out_ref[...] = attend(
            x, lambda *key: copies[key].wait(), wq_ref, k_ref, v_ref, wo_ref, b_ref, s_ref
        )

    shape = jax.ShapeDtypeStruct((rows, share * cols), BF)
    return pl.pallas_call(
        body,
        out_shape=(shape, shape, pltpu.VMEM(w_qkv.shape, BF), pltpu.VMEM(w_out.shape, BF)),
        in_specs=[VMEM_SPEC] * 3 + [HBM_SPEC] * 4,
        out_specs=(VMEM_SPEC,) * 4,
        scratch_shapes=[
            score_scratch(rows, pages, page_len, share),
            pltpu.VMEM(key_cache.shape[1:], BF),
            pltpu.VMEM(value_cache.shape[1:], BF),
            pltpu.SemaphoreType.DMA((parts,)),
            pltpu.SemaphoreType.DMA((parts,)),
            pltpu.SemaphoreType.DMA((4,)),
        ],
        compiler_params=pltpu.CompilerParams(vmem_limit_bytes=20 * MIB),
    )(incoming, take, bias, *map(in_place, (w_qkv, w_out, key_cache, value_cache)))


def norm_attention(parts, residual, gain_bias, w_qkv, w_out, keys, values, bias):
    count = len(parts)

    def body(*refs):
        part_refs, (res_ref, norm_ref, wq_ref, wo_ref, k_ref, v_ref, b_ref) = refs[:count], refs[count : count + 7]
        x_ref, out_ref, s_ref = refs[count + 7 :]
        x = add_norm([r[...] for r in part_refs], res_ref[...], norm_ref[...])
        x_ref[...] = x
        out_ref[...] = attend(x, lambda *key: None, wq_ref, k_ref, v_ref, wo_ref, b_ref, s_ref)

    shape = jax.ShapeDtypeStruct(residual.shape, BF)
    scratch = [score_scratch(residual.shape[0], *keys.shape)]
    return kernel_call(
        body, (shape, shape), scratch, 12, *parts, residual, gain_bias, w_qkv, w_out, keys, values, bias
    )


def norm_mlp(parts, residual, gain_bias, w_up, w_down):
    count = len(parts)

    def body(*refs):
        part_refs, (res_ref, norm_ref, up_ref, down_ref) = refs[:count], refs[count : count + 4]
        x_ref, out_ref = refs[count + 4 :]
        x = add_norm([r[...] for r in part_refs], res_ref[...], norm_ref[...])
        x_ref[...] = x
        up = jnp.dot(x, up_ref[...], preferred_element_type=F32)
        active = jax.nn.gelu(up, approximate=True).astype(BF)
        out_ref[...] = jnp.dot(active, down_ref[...], preferred_element_type=F32).astype(BF)

    shape = jax.ShapeDtypeStruct(residual.shape, BF)
    return kernel_call(body, (shape, shape), [], 8, *parts, residual, gain_bias, w_up, w_down)


def norm_send(parts, residual, gain_bias, give):
    count = len(parts)
    cols = give.shape[1] // residual.shape[0]
    share = residual.shape[1] // cols

    def body(*refs):
        res_ref, norm_ref, give_ref, out_ref = refs[count:]
        x = add_norm([r[...] for r in refs[:count]], res_ref[...], norm_ref[...])
        out_ref[...] = lay_out(give_ref[...], x, cols)

    shape = jax.ShapeDtypeStruct((give.shape[0], share), BF)
    return kernel_call(body, shape, [], 8, *parts, residual, gain_bias, give)


def lay_out(give, rows_here, cols):
    share = rows_here.shape[1] // cols
    stacked = jnp.concatenate([rows_here[:, c * share : (c + 1) * share] for c in range(cols)], axis=0)
    return jnp.dot(give, stacked, preferred_element_type=F32).astype(BF)


def gather_parts(part):
    size = lax.axis_size("tp")
    return [part] + [
        lax.ppermute(part, "tp", [(i, (i + step) % size) for i in range(size)])
        for step in range(1, size)
    ]


def iota(shape, dim):
    return lax.broadcasted_iota(jnp.int32, shape, dim)


def deal_send(order, tokens, blocks, cols):
    rows, width = tokens.shape
    lines, stack = blocks * CAP * cols, cols * rows

    def body(order_hbm, tok_hbm, out_ref, give_ref, order_ref, tok_ref, sems):
        order_copy = pltpu.make_async_copy(order_hbm, order_ref, sems.at[0])
        token_copy = pltpu.make_async_copy(tok_hbm, tok_ref, sems.at[1])
        order_copy.start()
        token_copy.start()
        first = lax.axis_index("req") * rows
        order_copy.wait()
        wanted = first + iota((stack, order.shape[1]), 0) % rows
        goes = jnp.concatenate(
            [(order_ref[r : r + 1, :] == wanted).astype(F32).astype(BF) for r in range(order.shape[0])], axis=1
        )
        slots = order.shape[0] * order.shape[1]
        block_of = (iota((blocks, slots), 1) // rows == iota((blocks, slots), 0)).astype(F32).astype(BF)
        sent = lax.dot_general(block_of, goes, (((1,), (1,)), ((), ())), preferred_element_type=F32)
        a, b = iota((stack, stack), 0), iota((stack, stack), 1)
        earlier = ((a // rows == b // rows) & (a < b)).astype(F32).astype(BF)
        rank = jnp.dot(sent.astype(BF), earlier, preferred_element_type=F32)
        line, block = iota((lines, blocks), 0), iota((lines, blocks), 1)
        give = jnp.zeros((lines, stack), F32)
        for k in range(CAP):
            spread = (line // cols == block * CAP + k).astype(F32).astype(BF)
            chosen = jnp.where(rank == k, sent, 0.0).astype(BF)
            give = give + jnp.dot(spread, chosen, preferred_element_type=F32)
        same = iota((lines, stack), 0) % cols == iota((lines, stack), 1) // rows
        give = jnp.where(same, give, 0.0)
        give_ref[...] = give
        token_copy.wait()
        out_ref[...] = lay_out(give.astype(BF), tok_ref[...], cols)

    return pl.pallas_call(
        body,
        out_shape=(jax.ShapeDtypeStruct((lines, width // cols), BF), jax.ShapeDtypeStruct((lines, stack), F32)),
        in_specs=[HBM_SPEC] * 2,
        out_specs=(VMEM_SPEC,) * 2,
        scratch_shapes=[
            pltpu.VMEM(order.shape, order.dtype),
            pltpu.VMEM(tokens.shape, BF),
            pltpu.SemaphoreType.DMA((2,)),
        ],
        compiler_params=pltpu.CompilerParams(vmem_limit_bytes=8 * MIB),
    )(in_place(order), in_place(tokens))


def deal_take(order, give, table, lengths, cols, pages, page_len):
    rows = lengths.shape[1]
    lines, stack = give.shape

    def body(order_ref, give_ref, table_ref, len_ref, take_ref, back_ref, send_ref, bias_ref):
        req = lax.axis_index("req")
        slot = req * rows + iota((stack, order.shape[1]), 0) % rows
        mine = jnp.zeros((stack, order.shape[1]), F32)
        for r in range(order.shape[0]):
            here = iota((stack, order.shape[1]), 1) + r * order.shape[1]
            mine = mine + jnp.where(here == slot, order_ref[r : r + 1, :], 0).astype(F32)
        column = jnp.broadcast_to(jnp.sum(mine, axis=1, keepdims=True), (stack, stack))
        line_of = jnp.transpose(column).astype(jnp.int32)
        column = column.astype(jnp.int32)
        a, b = iota((stack, stack), 0), iota((stack, stack), 1)
        before = (b < rows) & (column // rows == line_of // rows) & (line_of < column)
        rank = jnp.sum(before.astype(F32), axis=1, keepdims=True).astype(jnp.int32)
        place = (column[:, 0:1] // rows * CAP + rank) * cols + iota((stack, 1), 0) // rows
        take = (iota((stack, lines), 1) == place).astype(F32)
        take_ref[...] = take.astype(BF)
        send_ref[...] = jnp.transpose(take).astype(BF)
        back_ref[...] = jnp.transpose(give_ref[...]).astype(BF)
        diagonal = iota((rows, rows), 0) == iota((rows, rows), 1)

        def stand(line):
            return jnp.sum(jnp.where(diagonal, line, 0).astype(F32), axis=1, keepdims=True).astype(jnp.int32)

        length = stand(len_ref[...])
        page = iota((rows, page_len), 1) + req * pages
        room = jnp.zeros((rows, page_len), jnp.int32)
        for k in range(table.shape[0]):
            left = length - k * page_len
            hit = (stand(table_ref[k : k + 1, :]) == page) & (left > 0)
            room = room + jnp.where(hit, left, 0)
        offset = iota((rows, page_len), 1)
        for p in range(pages):
            bias_ref[:, p * page_len : (p + 1) * page_len] = jnp.where(
                offset < room[:, p : p + 1], 0.0, -jnp.inf
            ).astype(F32)

    out = (
        jax.ShapeDtypeStruct((stack, lines), BF),
        jax.ShapeDtypeStruct((stack, lines), BF),
        jax.ShapeDtypeStruct((lines, stack), BF),
        jax.ShapeDtypeStruct((rows, pages * page_len), F32),
    )
    return kernel_call(body, out, [], 8, order, give, table, lengths)


def settle(incoming, back, rows):
    cols = back.shape[0] // rows

    def body(in_ref, back_ref, out_ref):
        stacked = jnp.dot(back_ref[...], in_ref[...], preferred_element_type=F32).astype(BF)
        out_ref[...] = jnp.concatenate([stacked[c * rows : (c + 1) * rows] for c in range(cols)], axis=1)

    shape = jax.ShapeDtypeStruct((rows, incoming.shape[1] * cols), BF)
    return kernel_call(body, shape, [], 8, incoming, back)


def swap(lines_out, blocks):
    lines, share = lines_out.shape
    return lax.all_to_all(lines_out.reshape(blocks, lines // blocks, share), "req", 0, 0).reshape(lines, share)


def local(
    tokens,
    deal_order,
    page_table,
    lengths,
    qkv_weight,
    out_weight,
    up_weight,
    down_weight,
    key_cache,
    value_cache,
    attn_norm,
    mlp_norm,
):
    req_rows = tokens.shape[0]
    blocks = lax.axis_size("req")
    cols = lax.axis_size("tp")
    layers, pool_pages, page_len = key_cache.shape[:3]
    order = deal_order.reshape(-1, HD)
    outgoing, give = deal_send(order, tokens, blocks, cols)
    incoming = swap(outgoing, blocks)
    take, back, send, bias = deal_take(
        order, give, page_table.T, lengths.reshape(1, -1), cols, pool_pages, page_len
    )
    w_qkv = jnp.transpose(qkv_weight, (1, 0, 2))
    current, partial, w_qkv, w_out = first_attention(
        incoming, take, w_qkv, out_weight, key_cache, value_cache, bias
    )
    w_up, w_down, keys = load(partial, (up_weight, None), (down_weight, None), (key_cache, 1))
    for layer in range(layers):
        hidden, partial = norm_mlp(gather_parts(partial), current, attn_norm, w_up, w_down)
        if layer + 1 < layers:
            (values,) = load(partial, (value_cache, layer + 1))
            current, partial = norm_attention(
                gather_parts(partial), hidden, mlp_norm, w_qkv, w_out, keys, values, bias
            )
            if layer + 2 < layers:
                (keys,) = load(partial, (key_cache, layer + 2))
    leaving = norm_send(gather_parts(partial), hidden, mlp_norm, send)
    return settle(swap(leaving, blocks), back, req_rows)


def solution(mesh):
    in_specs = (
        P("req", None),
        P(),
        P("req", None),
        P("req"),
        P(None, None, "tp"),
        P("tp", None),
        P(None, "tp"),
        P("tp", None),
        P(None, "req", None, "tp"),
        P(None, "req", None, "tp"),
        P(),
        P(),
    )
    out_specs = P("req", None)
    return jax.shard_map(local, mesh=mesh, in_specs=in_specs, out_specs=out_specs, check_vma=False)
```

```python
import math

import jax
import jax.numpy as jnp
from jax import lax
from jax.experimental import pallas as pl
from jax.experimental.pallas import tpu as pltpu
from jax.sharding import PartitionSpec as P

HD = 128
CAP = 2
EPS = 1e-6
BF = jnp.bfloat16
F32 = jnp.float32
MIB = 1 << 20
DEPTH = 3
STEP = 7
VMEM_SPEC = pl.BlockSpec(memory_space=pltpu.VMEM)
HBM_SPEC = pl.BlockSpec(memory_space=pltpu.HBM)


def kernel_call(body, out_shape, scratch, limit_mib, *operands):
    return pl.pallas_call(
        body,
        out_shape=out_shape,
        in_specs=[VMEM_SPEC] * len(operands),
        out_specs=jax.tree.map(lambda _: VMEM_SPEC, out_shape),
        scratch_shapes=scratch,
        compiler_params=pltpu.CompilerParams(vmem_limit_bytes=limit_mib * MIB),
    )(*operands)


def in_place(array):
    return pltpu.with_memory_space_constraint(array, pltpu.HBM)


def add_norm(parts, residual, gain_bias):
    total = residual.astype(F32)
    for part in parts:
        total = total + part.astype(F32)
    width = total.shape[-1]
    row_mean = jnp.sum(total, axis=-1, keepdims=True) * (1.0 / width)
    centered = total - row_mean
    row_var = jnp.sum(centered * centered, axis=-1, keepdims=True) * (1.0 / width)
    return (centered * lax.rsqrt(row_var + EPS) * gain_bias[0:1, :] + gain_bias[1:2, :]).astype(BF)


def attend(x, wait, w_qkv, score, v_ref, w_out, bias, s_ref, step):
    rows = x.shape[0]
    share = w_qkv.shape[2]
    heads = share // HD
    pages, page_len = v_ref.shape[:2]
    span = step * page_len
    scale = 1.0 / math.sqrt(HD)
    projected = []
    for i in range(3):
        wait("qkv", i)
        projected.append(jnp.dot(x, w_qkv[i], preferred_element_type=F32).astype(BF))
    query, fresh_key, fresh_value = projected
    lane_head = lax.broadcasted_iota(jnp.int32, (rows, share), 1) // HD
    wide = jnp.concatenate(
        [jnp.where(lane_head == h, query.astype(F32), 0.0) for h in range(heads)], axis=0
    )
    own_key = jnp.concatenate([fresh_key.astype(F32)] * heads, axis=0)
    own = jnp.sum(wide * own_key, axis=-1, keepdims=True)
    wide = wide.astype(BF)
    peak = jnp.full((heads * rows, HD), -jnp.inf, F32)
    for c in range(pages // step):
        scores = score(wide, slice(c * span, (c + 1) * span))
        here = bias[:, c * span : (c + 1) * span]
        scores = scores + jnp.concatenate([here] * heads, axis=0)
        s_ref[:, c * span : (c + 1) * span] = scores
        for i in range(span // HD):
            peak = jnp.maximum(peak, scores[:, i * HD : (i + 1) * HD])
    peak = jnp.maximum(jnp.max(peak, axis=-1, keepdims=True), own)
    sums = jnp.zeros((heads * rows, HD), F32)
    mixed = jnp.zeros((heads * rows, share), F32)
    for c in range(pages // step):
        weight = jnp.exp((s_ref[:, c * span : (c + 1) * span] - peak) * scale)
        for i in range(span // HD):
            sums = sums + weight[:, i * HD : (i + 1) * HD]
        wait("value", c * step)
        values = v_ref[c * step : (c + 1) * step].reshape(span, share)
        mixed = mixed + jnp.dot(weight.astype(BF), values, preferred_element_type=F32)
    own_weight = jnp.exp((own - peak) * scale)
    total = jnp.sum(sums, axis=-1, keepdims=True) + own_weight
    fresh_value = fresh_value.astype(F32)
    own_weight = own_weight.astype(BF).astype(F32)
    attended = []
    for h in range(heads):
        r = slice(h * rows, (h + 1) * rows)
        f = slice(h * HD, (h + 1) * HD)
        attended.append((mixed[r, f] + own_weight[r] * fresh_value[:, f]) / total[r])
    attended = jnp.concatenate(attended, axis=1).astype(BF)
    wait("out", 0)
    return jnp.dot(attended, w_out[...], preferred_element_type=F32).astype(BF)


def k_step(pages):
    return math.gcd(pages, 21)


def score_scratch(rows, pages, page_len, share):
    return pltpu.VMEM((rows * share // HD, pages * page_len), F32)


def load(after, *sources):
    count = len(sources)

    def body(*refs):
        copies = [
            pltpu.make_async_copy(
                refs[1 + i] if layer is None else refs[1 + i].at[layer], refs[1 + count + i], refs[-1].at[i]
            )
            for i, (_, layer) in enumerate(sources)
        ]
        for copy in copies:
            copy.start()
        for copy in copies:
            copy.wait()

    shapes = [a.shape if layer is None else a.shape[1:] for a, layer in sources]
    return pl.pallas_call(
        body,
        out_shape=tuple(pltpu.VMEM(shape, BF) for shape in shapes),
        in_specs=[HBM_SPEC] * (1 + count),
        out_specs=(VMEM_SPEC,) * count,
        scratch_shapes=[pltpu.SemaphoreType.DMA((count,))],
        compiler_params=pltpu.CompilerParams(vmem_limit_bytes=MIB),
        cost_estimate=load_cost(shapes),
    )(after, *(in_place(a) for a, _ in sources))


def load_cost(shapes):
    size = sum(2 * math.prod(shape) for shape in shapes)
    return pl.CostEstimate(flops=0, transcendentals=0, bytes_accessed=2 * size)


def load_turned(after, key_cache, layer):
    pages, page_len, share = key_cache.shape[1:]
    step = math.gcd(pages, 14)
    parts = pages // step
    span = step * page_len

    def body(after_ref, k_hbm, out_ref, k_ref, sems):
        copies = [
            pltpu.make_async_copy(k_hbm.at[layer, pl.ds(c * step, step)], k_ref.at[pl.ds(c * step, step)], sems.at[c])
            for c in range(parts)
        ]
        for copy in copies[:3]:
            copy.start()
        for c in range(parts):
            copies[c].wait()
            if c + 3 < parts:
                copies[c + 3].start()
            keys = k_ref[c * step : (c + 1) * step].reshape(span, share)
            out_ref[:, c * span : (c + 1) * span] = jnp.transpose(keys)

    return pl.pallas_call(
        body,
        out_shape=pltpu.VMEM((share, pages * page_len), BF),
        in_specs=[HBM_SPEC] * 2,
        out_specs=VMEM_SPEC,
        scratch_shapes=[pltpu.VMEM((pages, page_len, share), BF), pltpu.SemaphoreType.DMA((parts,))],
        compiler_params=pltpu.CompilerParams(vmem_limit_bytes=10 * MIB),
        cost_estimate=load_cost([key_cache.shape[1:]]),
    )(after, in_place(key_cache))


def first_attention(incoming, take, w_qkv, w_out, key_cache, value_cache, bias):
    rows = bias.shape[0]
    lines, share = incoming.shape
    cols = take.shape[0] // rows

    pages, page_len = key_cache.shape[1:3]
    step = k_step(pages)
    parts = pages // step
    span = step * page_len

    def body(in_ref, take_ref, b_ref, wq_hbm, wo_hbm, k_hbm, v_hbm, x_ref, out_ref, wq_ref, wo_ref,
             s_ref, k_ref, turned_ref, v_ref, k_sems, v_sems, w_sems):
        copies = {}
        for c in range(parts):
            at = pl.ds(c * step, step)
            copies["key", c] = pltpu.make_async_copy(k_hbm.at[0, at], k_ref.at[at], k_sems.at[c])
        for i in range(3):
            copies["qkv", i] = pltpu.make_async_copy(wq_hbm.at[i], wq_ref.at[i], w_sems.at[i])
        for c in range(parts):
            at = pl.ds(c * step, step)
            copies["value", c * step] = pltpu.make_async_copy(v_hbm.at[0, at], v_ref.at[at], v_sems.at[c])
        copies["out", 0] = pltpu.make_async_copy(wo_hbm, wo_ref, w_sems.at[3])
        order = list(copies)
        for key in order[:DEPTH]:
            copies[key].start()

        def wait(*key):
            if key not in copies:
                return
            copies[key].wait()
            later = order.index(key) + DEPTH
            if later < len(order):
                copies[order[later]].start()

        def score(wide, at):
            return jnp.dot(wide, turned_ref[:, at], preferred_element_type=F32)

        stacked = jnp.dot(take_ref[...], in_ref[...], preferred_element_type=F32).astype(BF)
        x = jnp.concatenate([stacked[c * rows : (c + 1) * rows] for c in range(cols)], axis=1)
        x_ref[...] = x
        for c in range(parts):
            wait("key", c)
            keys = k_ref[c * step : (c + 1) * step].reshape(span, share)
            turned_ref[:, c * span : (c + 1) * span] = jnp.transpose(keys)
        out_ref[...] = attend(x, wait, wq_ref, score, v_ref, wo_ref, b_ref, s_ref, math.gcd(step, STEP))

    shape = jax.ShapeDtypeStruct((rows, share * cols), BF)
    return pl.pallas_call(
        body,
        out_shape=(shape, shape, pltpu.VMEM(w_qkv.shape, BF), pltpu.VMEM(w_out.shape, BF)),
        in_specs=[VMEM_SPEC] * 3 + [HBM_SPEC] * 4,
        out_specs=(VMEM_SPEC,) * 4,
        scratch_shapes=[
            score_scratch(rows, pages, page_len, share),
            pltpu.VMEM(key_cache.shape[1:], BF),
            pltpu.VMEM((share, pages * page_len), BF),
            pltpu.VMEM(value_cache.shape[1:], BF),
            pltpu.SemaphoreType.DMA((parts,)),
            pltpu.SemaphoreType.DMA((parts,)),
            pltpu.SemaphoreType.DMA((4,)),
        ],
        compiler_params=pltpu.CompilerParams(vmem_limit_bytes=24 * MIB),
    )(incoming, take, bias, *map(in_place, (w_qkv, w_out, key_cache, value_cache)))


def norm_attention(parts, residual, gain_bias, w_qkv, w_out, keys, values, bias):
    count = len(parts)
    step = math.gcd(values.shape[0], 6)

    def body(*refs):
        part_refs, (res_ref, norm_ref, wq_ref, wo_ref, k_ref, v_ref, b_ref) = refs[:count], refs[count : count + 7]
        x_ref, out_ref, s_ref = refs[count + 7 :]
        x = add_norm([r[...] for r in part_refs], res_ref[...], norm_ref[...])
        x_ref[...] = x

        def score(wide, at):
            return jnp.dot(wide, k_ref[:, at], preferred_element_type=F32)

        out_ref[...] = attend(x, lambda *key: None, wq_ref, score, v_ref, wo_ref, b_ref, s_ref, step)

    shape = jax.ShapeDtypeStruct(residual.shape, BF)
    scratch = [score_scratch(residual.shape[0], *values.shape)]
    return kernel_call(
        body, (shape, shape), scratch, 12, *parts, residual, gain_bias, w_qkv, w_out, keys, values, bias
    )


def norm_mlp(parts, residual, gain_bias, w_up, w_down):
    count = len(parts)

    def body(*refs):
        part_refs, (res_ref, norm_ref, up_ref, down_ref) = refs[:count], refs[count : count + 4]
        x_ref, out_ref = refs[count + 4 :]
        x = add_norm([r[...] for r in part_refs], res_ref[...], norm_ref[...])
        x_ref[...] = x
        up = jnp.dot(x, up_ref[...], preferred_element_type=F32)
        active = jax.nn.gelu(up, approximate=True).astype(BF)
        out_ref[...] = jnp.dot(active, down_ref[...], preferred_element_type=F32).astype(BF)

    shape = jax.ShapeDtypeStruct(residual.shape, BF)
    return kernel_call(body, (shape, shape), [], 8, *parts, residual, gain_bias, w_up, w_down)


def norm_send(parts, residual, gain_bias, give):
    count = len(parts)
    cols = give.shape[1] // residual.shape[0]
    share = residual.shape[1] // cols

    def body(*refs):
        res_ref, norm_ref, give_ref, out_ref = refs[count:]
        x = add_norm([r[...] for r in refs[:count]], res_ref[...], norm_ref[...])
        out_ref[...] = lay_out(give_ref[...], x, cols)

    shape = jax.ShapeDtypeStruct((give.shape[0], share), BF)
    return kernel_call(body, shape, [], 8, *parts, residual, gain_bias, give)


def lay_out(give, rows_here, cols):
    share = rows_here.shape[1] // cols
    stacked = jnp.concatenate([rows_here[:, c * share : (c + 1) * share] for c in range(cols)], axis=0)
    return jnp.dot(give, stacked, preferred_element_type=F32).astype(BF)


def gather_parts(part):
    size = lax.axis_size("tp")
    return [part] + [
        lax.ppermute(part, "tp", [(i, (i + step) % size) for i in range(size)])
        for step in range(1, size)
    ]


def iota(shape, dim):
    return lax.broadcasted_iota(jnp.int32, shape, dim)


def deal_send(order, tokens, blocks, cols):
    rows, width = tokens.shape
    lines, stack = blocks * CAP * cols, cols * rows
    groups, lanes = order.shape
    near = lanes // rows * CAP * cols

    def body(order_hbm, tok_hbm, out_ref, back_ref, order_ref, tok_ref, sems):
        order_copy = pltpu.make_async_copy(order_hbm, order_ref, sems.at[0])
        token_copy = pltpu.make_async_copy(tok_hbm, tok_ref, sems.at[1])
        order_copy.start()
        token_copy.start()
        wanted = lax.axis_index("req") * rows + iota((rows, lanes), 0)
        spread = iota((lanes, lines), 0) // rows == iota((lanes, lines), 1) % near // (CAP * cols)
        spread = spread.astype(F32).astype(BF)
        line = iota((rows, lines), 1)
        earlier = (iota((rows, rows), 1) < iota((rows, rows), 0)).astype(F32).astype(BF)
        order_copy.wait()
        goes = jnp.concatenate(
            [(order_ref[r : r + 1, :] == wanted).astype(F32).astype(BF) for r in range(groups)], axis=0
        )
        sent_by_group = jnp.dot(goes, spread, preferred_element_type=F32)
        sent = jnp.zeros((rows, lines), F32)
        for r in range(groups):
            sent = jnp.where(line // near == r, sent_by_group[r * rows : (r + 1) * rows], sent)
        rank = jnp.dot(earlier, sent.astype(BF), preferred_element_type=F32).astype(jnp.int32)
        mine = jnp.where(rank == line // cols % CAP, sent, 0.0)
        back = jnp.concatenate([jnp.where(line % cols == c, mine, 0.0) for c in range(cols)], axis=0)
        back_ref[...] = back.astype(BF)
        token_copy.wait()
        out_ref[...] = lay_out(jnp.transpose(back).astype(BF), tok_ref[...], cols)

    return pl.pallas_call(
        body,
        out_shape=(
            jax.ShapeDtypeStruct((lines, width // cols), BF),
            jax.ShapeDtypeStruct((stack, lines), BF),
        ),
        in_specs=[HBM_SPEC] * 2,
        out_specs=(VMEM_SPEC,) * 2,
        scratch_shapes=[
            pltpu.VMEM(order.shape, order.dtype),
            pltpu.VMEM(tokens.shape, BF),
            pltpu.SemaphoreType.DMA((2,)),
        ],
        compiler_params=pltpu.CompilerParams(vmem_limit_bytes=8 * MIB),
    )(in_place(order), in_place(tokens))


def deal_take(order, table, lengths, blocks, cols, pages, page_len):
    rows = lengths.shape[1]
    lines, stack = blocks * CAP * cols, cols * rows

    def body(order_ref, table_ref, len_ref, take_ref, send_ref, bias_ref):
        req = lax.axis_index("req")
        slot = req * rows + iota((stack, order.shape[1]), 0) % rows
        mine = jnp.zeros((stack, order.shape[1]), F32)
        for r in range(order.shape[0]):
            here = iota((stack, order.shape[1]), 1) + r * order.shape[1]
            mine = mine + jnp.where(here == slot, order_ref[r : r + 1, :], 0).astype(F32)
        column = jnp.broadcast_to(jnp.sum(mine, axis=1, keepdims=True), (stack, stack))
        line_of = jnp.transpose(column).astype(jnp.int32)
        column = column.astype(jnp.int32)
        a, b = iota((stack, stack), 0), iota((stack, stack), 1)
        before = (b < rows) & (column // rows == line_of // rows) & (line_of < column)
        rank = jnp.sum(before.astype(F32), axis=1, keepdims=True).astype(jnp.int32)
        place = (column[:, 0:1] // rows * CAP + rank) * cols + iota((stack, 1), 0) // rows
        take = (iota((stack, lines), 1) == place).astype(F32)
        take_ref[...] = take.astype(BF)
        send_ref[...] = jnp.transpose(take).astype(BF)
        diagonal = iota((rows, rows), 0) == iota((rows, rows), 1)

        def stand(line):
            return jnp.sum(jnp.where(diagonal, line, 0).astype(F32), axis=1, keepdims=True).astype(jnp.int32)

        length = stand(len_ref[...])
        page = iota((rows, page_len), 1) + req * pages
        room = jnp.zeros((rows, page_len), jnp.int32)
        for k in range(table.shape[0]):
            left = length - k * page_len
            hit = (stand(table_ref[k : k + 1, :]) == page) & (left > 0)
            room = room + jnp.where(hit, left, 0)
        offset = iota((rows, page_len), 1)
        for p in range(pages):
            bias_ref[:, p * page_len : (p + 1) * page_len] = jnp.where(
                offset < room[:, p : p + 1], 0.0, -jnp.inf
            ).astype(F32)

    out = (
        jax.ShapeDtypeStruct((stack, lines), BF),
        jax.ShapeDtypeStruct((lines, stack), BF),
        jax.ShapeDtypeStruct((rows, pages * page_len), F32),
    )
    return kernel_call(body, out, [], 8, order, table, lengths)


def settle(incoming, back, rows):
    cols = back.shape[0] // rows

    def body(in_ref, back_ref, out_ref):
        stacked = jnp.dot(back_ref[...], in_ref[...], preferred_element_type=F32).astype(BF)
        out_ref[...] = jnp.concatenate([stacked[c * rows : (c + 1) * rows] for c in range(cols)], axis=1)

    shape = jax.ShapeDtypeStruct((rows, incoming.shape[1] * cols), BF)
    return kernel_call(body, shape, [], 8, incoming, back)


def swap(lines_out, blocks):
    lines, share = lines_out.shape
    return lax.all_to_all(lines_out.reshape(blocks, lines // blocks, share), "req", 0, 0).reshape(lines, share)


def local(
    tokens,
    deal_order,
    page_table,
    lengths,
    qkv_weight,
    out_weight,
    up_weight,
    down_weight,
    key_cache,
    value_cache,
    attn_norm,
    mlp_norm,
):
    req_rows = tokens.shape[0]
    blocks = lax.axis_size("req")
    cols = lax.axis_size("tp")
    layers, pool_pages, page_len = key_cache.shape[:3]
    order = deal_order.reshape(-1, HD)
    outgoing, back = deal_send(order, tokens, blocks, cols)
    incoming = swap(outgoing, blocks)
    take, send, bias = deal_take(
        order, page_table.T, lengths.reshape(1, -1), blocks, cols, pool_pages, page_len
    )
    w_qkv = jnp.transpose(qkv_weight, (1, 0, 2))
    current, partial, w_qkv, w_out = first_attention(
        incoming, take, w_qkv, out_weight, key_cache, value_cache, bias
    )
    w_up, w_down, values = load(partial, (up_weight, None), (down_weight, None), (value_cache, 1))
    for layer in range(layers):
        hidden, partial = norm_mlp(gather_parts(partial), current, attn_norm, w_up, w_down)
        if layer + 1 < layers:
            keys = load_turned(partial, key_cache, layer + 1)
            current, partial = norm_attention(
                gather_parts(partial), hidden, mlp_norm, w_qkv, w_out, keys, values, bias
            )
            if layer + 2 < layers:
                (values,) = load(partial, (value_cache, layer + 2))
    leaving = norm_send(gather_parts(partial), hidden, mlp_norm, send)
    return settle(swap(leaving, blocks), back, req_rows)


def solution(mesh):
    in_specs = (
        P("req", None),
        P(),
        P("req", None),
        P("req"),
        P(None, None, "tp"),
        P("tp", None),
        P(None, "tp"),
        P("tp", None),
        P(None, "req", None, "tp"),
        P(None, "req", None, "tp"),
        P(),
        P(),
    )
    out_specs = P("req", None)
    return jax.shard_map(local, mesh=mesh, in_specs=in_specs, out_specs=out_specs, check_vma=False)
```

```python
import math

import jax
import jax.numpy as jnp
from jax import lax
from jax.experimental import pallas as pl
from jax.experimental.pallas import tpu as pltpu
from jax.sharding import PartitionSpec as P

HD = 128
CAP = 2
EPS = 1e-6
BF = jnp.bfloat16
F32 = jnp.float32
MIB = 1 << 20
DEPTH = 4
STEP = 7
SPLIT = 1
VMEM_SPEC = pl.BlockSpec(memory_space=pltpu.VMEM)
HBM_SPEC = pl.BlockSpec(memory_space=pltpu.HBM)


def kernel_call(body, out_shape, scratch, limit_mib, *operands):
    return pl.pallas_call(
        body,
        out_shape=out_shape,
        in_specs=[VMEM_SPEC] * len(operands),
        out_specs=jax.tree.map(lambda _: VMEM_SPEC, out_shape),
        scratch_shapes=scratch,
        compiler_params=pltpu.CompilerParams(vmem_limit_bytes=limit_mib * MIB),
    )(*operands)


def in_place(array):
    return pltpu.with_memory_space_constraint(array, pltpu.HBM)


def add_norm(parts, residual, gain_bias):
    total = residual.astype(F32)
    for part in parts:
        total = total + part.astype(F32)
    width = total.shape[-1]
    row_mean = jnp.sum(total, axis=-1, keepdims=True) * (1.0 / width)
    centered = total - row_mean
    row_var = jnp.sum(centered * centered, axis=-1, keepdims=True) * (1.0 / width)
    return (centered * lax.rsqrt(row_var + EPS) * gain_bias[0:1, :] + gain_bias[1:2, :]).astype(BF)


def attend(x, wait, project, share, score, v_ref, w_out, bias, s_ref, step):
    rows = x.shape[0]
    heads = share // HD
    pages, page_len = v_ref.shape[:2]
    span = step * page_len
    scale = math.log2(math.e) / math.sqrt(HD)
    query, fresh_key, fresh_value = (project(x, i).astype(BF) for i in range(3))
    lane_head = lax.broadcasted_iota(jnp.int32, (rows, share), 1) // HD
    wide = jnp.concatenate(
        [jnp.where(lane_head == h, query.astype(F32), 0.0) for h in range(heads)], axis=0
    )
    own_key = jnp.concatenate([fresh_key.astype(F32)] * heads, axis=0)
    own = jnp.sum(wide * own_key, axis=-1, keepdims=True)
    wide = wide.astype(BF)
    peak = jnp.full((heads * rows, HD), -jnp.inf, F32)
    for c in range(pages // step):
        scores = score(wide, slice(c * span, (c + 1) * span))
        here = bias[:, c * span : (c + 1) * span]
        scores = scores + jnp.concatenate([here] * heads, axis=0)
        s_ref[:, c * span : (c + 1) * span] = scores
        for i in range(span // HD):
            peak = jnp.maximum(peak, scores[:, i * HD : (i + 1) * HD])
    peak = jnp.maximum(jnp.max(peak, axis=-1, keepdims=True), own)
    sums = jnp.zeros((heads * rows, HD), F32)
    mixed = jnp.zeros((heads * rows, share), F32)
    for c in range(pages // step):
        weight = jnp.exp2((s_ref[:, c * span : (c + 1) * span] - peak) * scale)
        for i in range(span // HD):
            sums = sums + weight[:, i * HD : (i + 1) * HD]
        wait("value", c * step)
        values = v_ref[c * step : (c + 1) * step].reshape(span, share)
        mixed = mixed + jnp.dot(weight.astype(BF), values, preferred_element_type=F32)
    own_weight = jnp.exp2((own - peak) * scale)
    total = jnp.sum(sums, axis=-1, keepdims=True) + own_weight
    fresh_value = fresh_value.astype(F32)
    own_weight = own_weight.astype(BF).astype(F32)
    attended = []
    for h in range(heads):
        r = slice(h * rows, (h + 1) * rows)
        f = slice(h * HD, (h + 1) * HD)
        attended.append((mixed[r, f] + own_weight[r] * fresh_value[:, f]) / total[r])
    attended = jnp.concatenate(attended, axis=1).astype(BF)
    return jnp.dot(attended, w_out[...], preferred_element_type=F32).astype(BF)


def k_step(pages):
    return math.gcd(pages, 21)


def score_scratch(rows, pages, page_len, share):
    return pltpu.VMEM((rows * share // HD, pages * page_len), F32)


def load(after, *sources):
    count = len(sources)

    def body(*refs):
        copies = [
            pltpu.make_async_copy(
                refs[1 + i] if layer is None else refs[1 + i].at[layer], refs[1 + count + i], refs[-1].at[i]
            )
            for i, (_, layer) in enumerate(sources)
        ]
        for copy in copies:
            copy.start()
        for copy in copies:
            copy.wait()

    shapes = [a.shape if layer is None else a.shape[1:] for a, layer in sources]
    return pl.pallas_call(
        body,
        out_shape=tuple(pltpu.VMEM(shape, BF) for shape in shapes),
        in_specs=[HBM_SPEC] * (1 + count),
        out_specs=(VMEM_SPEC,) * count,
        scratch_shapes=[pltpu.SemaphoreType.DMA((count,))],
        compiler_params=pltpu.CompilerParams(vmem_limit_bytes=MIB),
        cost_estimate=load_cost(shapes),
    )(after, *(in_place(a) for a, _ in sources))


def load_cost(shapes):
    size = sum(2 * math.prod(shape) for shape in shapes)
    return pl.CostEstimate(flops=0, transcendentals=0, bytes_accessed=2 * size)


def load_turned(after, key_cache, layer):
    pages, page_len, share = key_cache.shape[1:]
    step = math.gcd(pages, 14)
    parts = pages // step
    span = step * page_len

    def body(after_ref, k_hbm, out_ref, k_ref, sems):
        copies = [
            pltpu.make_async_copy(k_hbm.at[layer, pl.ds(c * step, step)], k_ref.at[pl.ds(c * step, step)], sems.at[c])
            for c in range(parts)
        ]
        for copy in copies[:3]:
            copy.start()
        for c in range(parts):
            copies[c].wait()
            if c + 3 < parts:
                copies[c + 3].start()
            keys = k_ref[c * step : (c + 1) * step].reshape(span, share)
            out_ref[:, c * span : (c + 1) * span] = jnp.transpose(keys)

    return pl.pallas_call(
        body,
        out_shape=pltpu.VMEM((share, pages * page_len), BF),
        in_specs=[HBM_SPEC] * 2,
        out_specs=VMEM_SPEC,
        scratch_shapes=[pltpu.VMEM((pages, page_len, share), BF), pltpu.SemaphoreType.DMA((parts,))],
        compiler_params=pltpu.CompilerParams(vmem_limit_bytes=10 * MIB),
        cost_estimate=load_cost([key_cache.shape[1:]]),
    )(after, in_place(key_cache))


def first_attention(incoming, take, w_qkv, w_out, key_cache, value_cache, bias):
    rows = bias.shape[0]
    lines, share = incoming.shape
    cols = take.shape[0] // rows

    pages, page_len = key_cache.shape[1:3]
    step = k_step(pages)
    parts = pages // step
    piece = w_qkv.shape[1] // SPLIT

    def body(in_ref, take_ref, b_ref, wo_ref, wq_hbm, k_hbm, v_hbm, x_ref, out_ref, wq_ref,
             s_ref, k_ref, v_ref, k_sems, v_sems, w_sems):
        copies = {}
        for i in range(3):
            for c in range(SPLIT):
                at = pl.ds(c * piece, piece)
                copies["qkv", i, c] = pltpu.make_async_copy(
                    wq_hbm.at[i, at], wq_ref.at[i, at], w_sems.at[i * SPLIT + c]
                )
        for c in range(parts):
            at = pl.ds(c * step, step)
            copies["key", c * step] = pltpu.make_async_copy(k_hbm.at[0, at], k_ref.at[at], k_sems.at[c])
        for c in range(parts):
            at = pl.ds(c * step, step)
            copies["value", c * step] = pltpu.make_async_copy(v_hbm.at[0, at], v_ref.at[at], v_sems.at[c])
        order = list(copies)
        for key in order[:DEPTH]:
            copies[key].start()

        def wait(*key):
            if key not in copies:
                return
            copies[key].wait()
            later = order.index(key) + DEPTH
            if later < len(order):
                copies[order[later]].start()

        def score(wide, at):
            wait("key", at.start // page_len)
            keys = k_ref[at.start // page_len : at.stop // page_len].reshape(at.stop - at.start, share)
            return lax.dot_general(wide, keys, (((1,), (1,)), ((), ())), preferred_element_type=F32)

        def project(x, i):
            total = None
            for c in range(SPLIT):
                wait("qkv", i, c)
                at = slice(c * piece, (c + 1) * piece)
                term = jnp.dot(x[:, at], wq_ref[i, at], preferred_element_type=F32)
                total = term if total is None else total + term
            return total

        stacked = jnp.dot(take_ref[...], in_ref[...], preferred_element_type=F32).astype(BF)
        x = jnp.concatenate([stacked[c * rows : (c + 1) * rows] for c in range(cols)], axis=1)
        x_ref[...] = x
        out_ref[...] = attend(x, wait, project, share, score, v_ref, wo_ref, b_ref, s_ref, math.gcd(step, STEP))

    shape = jax.ShapeDtypeStruct((rows, share * cols), BF)
    return pl.pallas_call(
        body,
        out_shape=(shape, shape, pltpu.VMEM(w_qkv.shape, BF)),
        in_specs=[VMEM_SPEC] * 4 + [HBM_SPEC] * 3,
        out_specs=(VMEM_SPEC,) * 3,
        scratch_shapes=[
            score_scratch(rows, pages, page_len, share),
            pltpu.VMEM(key_cache.shape[1:], BF),
            pltpu.VMEM(value_cache.shape[1:], BF),
            pltpu.SemaphoreType.DMA((parts,)),
            pltpu.SemaphoreType.DMA((parts,)),
            pltpu.SemaphoreType.DMA((3 * SPLIT,)),
        ],
        compiler_params=pltpu.CompilerParams(vmem_limit_bytes=24 * MIB),
    )(incoming, take, bias, w_out, *map(in_place, (w_qkv, key_cache, value_cache)))


def norm_attention(parts, residual, gain_bias, w_qkv, w_out, keys, values, bias):
    count = len(parts)
    step = math.gcd(values.shape[0], 6)

    def body(*refs):
        part_refs, (res_ref, norm_ref, wq_ref, wo_ref, k_ref, v_ref, b_ref) = refs[:count], refs[count : count + 7]
        x_ref, out_ref, s_ref = refs[count + 7 :]
        x = add_norm([r[...] for r in part_refs], res_ref[...], norm_ref[...])
        x_ref[...] = x

        def score(wide, at):
            return jnp.dot(wide, k_ref[:, at], preferred_element_type=F32)

        def project(x, i):
            return jnp.dot(x, wq_ref[i], preferred_element_type=F32)

        out_ref[...] = attend(x, lambda *key: None, project, wq_ref.shape[2], score, v_ref, wo_ref, b_ref, s_ref, step)

    shape = jax.ShapeDtypeStruct(residual.shape, BF)
    scratch = [score_scratch(residual.shape[0], *values.shape)]
    return kernel_call(
        body, (shape, shape), scratch, 12, *parts, residual, gain_bias, w_qkv, w_out, keys, values, bias
    )


def norm_mlp(parts, residual, gain_bias, w_up, w_down):
    count = len(parts)

    def body(*refs):
        part_refs, (res_ref, norm_ref, up_ref, down_ref) = refs[:count], refs[count : count + 4]
        x_ref, out_ref = refs[count + 4 :]
        x = add_norm([r[...] for r in part_refs], res_ref[...], norm_ref[...])
        x_ref[...] = x
        up = jnp.dot(x, up_ref[...], preferred_element_type=F32)
        active = jax.nn.gelu(up, approximate=True).astype(BF)
        out_ref[...] = jnp.dot(active, down_ref[...], preferred_element_type=F32).astype(BF)

    shape = jax.ShapeDtypeStruct(residual.shape, BF)
    return kernel_call(body, (shape, shape), [], 8, *parts, residual, gain_bias, w_up, w_down)


def norm_send(parts, residual, gain_bias, give):
    count = len(parts)
    cols = give.shape[1] // residual.shape[0]
    share = residual.shape[1] // cols

    def body(*refs):
        res_ref, norm_ref, give_ref, out_ref = refs[count:]
        x = add_norm([r[...] for r in refs[:count]], res_ref[...], norm_ref[...])
        out_ref[...] = lay_out(give_ref[...], x, cols)

    shape = jax.ShapeDtypeStruct((give.shape[0], share), BF)
    return kernel_call(body, shape, [], 8, *parts, residual, gain_bias, give)


def lay_out(give, rows_here, cols):
    share = rows_here.shape[1] // cols
    stacked = jnp.concatenate([rows_here[:, c * share : (c + 1) * share] for c in range(cols)], axis=0)
    return jnp.dot(give, stacked, preferred_element_type=F32).astype(BF)


def gather_parts(part):
    size = lax.axis_size("tp")
    return [part] + [
        lax.ppermute(part, "tp", [(i, (i + step) % size) for i in range(size)])
        for step in range(1, size)
    ]


def iota(shape, dim):
    return lax.broadcasted_iota(jnp.int32, shape, dim)


def deal_send(order, tokens, blocks, cols):
    rows, width = tokens.shape
    lines, stack = blocks * CAP * cols, cols * rows
    groups, lanes = order.shape
    near = lanes // rows * CAP * cols

    def body(order_hbm, tok_hbm, out_ref, back_ref, order_ref, tok_ref, sems):
        order_copy = pltpu.make_async_copy(order_hbm, order_ref, sems.at[0])
        token_copy = pltpu.make_async_copy(tok_hbm, tok_ref, sems.at[1])
        order_copy.start()
        token_copy.start()
        wanted = lax.axis_index("req") * rows + iota((rows, lanes), 0)
        spread = iota((lanes, lines), 0) // rows == iota((lanes, lines), 1) % near // (CAP * cols)
        spread = spread.astype(F32).astype(BF)
        line = iota((rows, lines), 1)
        earlier = (iota((rows, rows), 1) < iota((rows, rows), 0)).astype(F32).astype(BF)
        order_copy.wait()
        goes = jnp.concatenate(
            [(order_ref[r : r + 1, :] == wanted).astype(F32).astype(BF) for r in range(groups)], axis=0
        )
        sent_by_group = jnp.dot(goes, spread, preferred_element_type=F32)
        sent = jnp.zeros((rows, lines), F32)
        for r in range(groups):
            sent = jnp.where(line // near == r, sent_by_group[r * rows : (r + 1) * rows], sent)
        rank = jnp.dot(earlier, sent.astype(BF), preferred_element_type=F32).astype(jnp.int32)
        mine = jnp.where(rank == line // cols % CAP, sent, 0.0)
        back = jnp.concatenate([jnp.where(line % cols == c, mine, 0.0) for c in range(cols)], axis=0)
        back_ref[...] = back.astype(BF)
        token_copy.wait()
        out_ref[...] = lay_out(jnp.transpose(back).astype(BF), tok_ref[...], cols)

    return pl.pallas_call(
        body,
        out_shape=(
            jax.ShapeDtypeStruct((lines, width // cols), BF),
            jax.ShapeDtypeStruct((stack, lines), BF),
        ),
        in_specs=[HBM_SPEC] * 2,
        out_specs=(VMEM_SPEC,) * 2,
        scratch_shapes=[
            pltpu.VMEM(order.shape, order.dtype),
            pltpu.VMEM(tokens.shape, BF),
            pltpu.SemaphoreType.DMA((2,)),
        ],
        compiler_params=pltpu.CompilerParams(vmem_limit_bytes=8 * MIB),
    )(in_place(order), in_place(tokens))


def deal_take(order, table, lengths, w_out, blocks, cols, pages, page_len):
    rows = lengths.shape[1]
    lines, stack = blocks * CAP * cols, cols * rows

    def body(order_ref, table_ref, len_ref, wo_hbm, take_ref, send_ref, bias_ref, wo_ref, sem):
        copy = pltpu.make_async_copy(wo_hbm, wo_ref, sem)
        copy.start()
        req = lax.axis_index("req")
        slot = req * rows + iota((stack, order.shape[1]), 0) % rows
        mine = jnp.zeros((stack, order.shape[1]), F32)
        for r in range(order.shape[0]):
            here = iota((stack, order.shape[1]), 1) + r * order.shape[1]
            mine = mine + jnp.where(here == slot, order_ref[r : r + 1, :], 0).astype(F32)
        column = jnp.broadcast_to(jnp.sum(mine, axis=1, keepdims=True), (stack, stack))
        line_of = jnp.transpose(column).astype(jnp.int32)
        column = column.astype(jnp.int32)
        a, b = iota((stack, stack), 0), iota((stack, stack), 1)
        before = (b < rows) & (column // rows == line_of // rows) & (line_of < column)
        rank = jnp.sum(before.astype(F32), axis=1, keepdims=True).astype(jnp.int32)
        place = (column[:, 0:1] // rows * CAP + rank) * cols + iota((stack, 1), 0) // rows
        take = (iota((stack, lines), 1) == place).astype(F32)
        take_ref[...] = take.astype(BF)
        send_ref[...] = jnp.transpose(take).astype(BF)
        diagonal = iota((rows, rows), 0) == iota((rows, rows), 1)

        def stand(line):
            return jnp.sum(jnp.where(diagonal, line, 0).astype(F32), axis=1, keepdims=True).astype(jnp.int32)

        length = stand(len_ref[...])
        page = iota((rows, page_len), 1) + req * pages
        room = jnp.zeros((rows, page_len), jnp.int32)
        for k in range(table.shape[0]):
            left = length - k * page_len
            hit = (stand(table_ref[k : k + 1, :]) == page) & (left > 0)
            room = room + jnp.where(hit, left, 0)
        offset = iota((rows, page_len), 1)
        for p in range(pages):
            bias_ref[:, p * page_len : (p + 1) * page_len] = jnp.where(
                offset < room[:, p : p + 1], 0.0, -jnp.inf
            ).astype(F32)
        copy.wait()

    out = (
        jax.ShapeDtypeStruct((stack, lines), BF),
        jax.ShapeDtypeStruct((lines, stack), BF),
        jax.ShapeDtypeStruct((rows, pages * page_len), F32),
        pltpu.VMEM(w_out.shape, BF),
    )
    return pl.pallas_call(
        body,
        out_shape=out,
        in_specs=[VMEM_SPEC] * 3 + [HBM_SPEC],
        out_specs=(VMEM_SPEC,) * 4,
        scratch_shapes=[pltpu.SemaphoreType.DMA],
        compiler_params=pltpu.CompilerParams(vmem_limit_bytes=8 * MIB),
    )(order, table, lengths, in_place(w_out))


def settle(incoming, back, rows):
    cols = back.shape[0] // rows

    def body(in_ref, back_ref, out_ref):
        stacked = jnp.dot(back_ref[...], in_ref[...], preferred_element_type=F32).astype(BF)
        out_ref[...] = jnp.concatenate([stacked[c * rows : (c + 1) * rows] for c in range(cols)], axis=1)

    shape = jax.ShapeDtypeStruct((rows, incoming.shape[1] * cols), BF)
    return kernel_call(body, shape, [], 8, incoming, back)


def swap(lines_out, blocks):
    lines, share = lines_out.shape
    return lax.all_to_all(lines_out.reshape(blocks, lines // blocks, share), "req", 0, 0).reshape(lines, share)


def local(
    tokens,
    deal_order,
    page_table,
    lengths,
    qkv_weight,
    out_weight,
    up_weight,
    down_weight,
    key_cache,
    value_cache,
    attn_norm,
    mlp_norm,
):
    req_rows = tokens.shape[0]
    blocks = lax.axis_size("req")
    cols = lax.axis_size("tp")
    layers, pool_pages, page_len = key_cache.shape[:3]
    order = deal_order.reshape(-1, HD)
    outgoing, back = deal_send(order, tokens, blocks, cols)
    incoming = swap(outgoing, blocks)
    take, send, bias, w_out = deal_take(
        order, page_table.T, lengths.reshape(1, -1), out_weight, blocks, cols, pool_pages, page_len
    )
    w_qkv = jnp.transpose(qkv_weight, (1, 0, 2))
    current, partial, w_qkv = first_attention(incoming, take, w_qkv, w_out, key_cache, value_cache, bias)
    w_up, w_down, values = load(partial, (up_weight, None), (down_weight, None), (value_cache, 1))
    for layer in range(layers):
        hidden, partial = norm_mlp(gather_parts(partial), current, attn_norm, w_up, w_down)
        if layer + 1 < layers:
            keys = load_turned(partial, key_cache, layer + 1)
            current, partial = norm_attention(
                gather_parts(partial), hidden, mlp_norm, w_qkv, w_out, keys, values, bias
            )
            if layer + 2 < layers:
                (values,) = load(partial, (value_cache, layer + 2))
    leaving = norm_send(gather_parts(partial), hidden, mlp_norm, send)
    return settle(swap(leaving, blocks), back, req_rows)


def solution(mesh):
    in_specs = (
        P("req", None),
        P(),
        P("req", None),
        P("req"),
        P(None, None, "tp"),
        P("tp", None),
        P(None, "tp"),
        P("tp", None),
        P(None, "req", None, "tp"),
        P(None, "req", None, "tp"),
        P(),
        P(),
    )
    out_specs = P("req", None)
    return jax.shard_map(local, mesh=mesh, in_specs=in_specs, out_specs=out_specs, check_vma=False)
```

```python
import math

import jax
import jax.numpy as jnp
from jax import lax
from jax.experimental import pallas as pl
from jax.experimental.pallas import tpu as pltpu
from jax.sharding import PartitionSpec as P

HD = 128
CAP = 2
EPS = 1e-6
BF = jnp.bfloat16
F32 = jnp.float32
MIB = 1 << 20
DEPTH = 4
STEP = 7
SPLIT = 1
VMEM_SPEC = pl.BlockSpec(memory_space=pltpu.VMEM)
HBM_SPEC = pl.BlockSpec(memory_space=pltpu.HBM)


def kernel_call(body, out_shape, scratch, limit_mib, *operands):
    return pl.pallas_call(
        body,
        out_shape=out_shape,
        in_specs=[VMEM_SPEC] * len(operands),
        out_specs=jax.tree.map(lambda _: VMEM_SPEC, out_shape),
        scratch_shapes=scratch,
        compiler_params=pltpu.CompilerParams(vmem_limit_bytes=limit_mib * MIB),
    )(*operands)


def in_place(array):
    return pltpu.with_memory_space_constraint(array, pltpu.HBM)


def add_norm(parts, residual, gain_bias):
    total = residual.astype(F32)
    for part in parts:
        total = total + part.astype(F32)
    width = total.shape[-1]
    row_mean = jnp.sum(total, axis=-1, keepdims=True) * (1.0 / width)
    centered = total - row_mean
    row_var = jnp.sum(centered * centered, axis=-1, keepdims=True) * (1.0 / width)
    return (centered * lax.rsqrt(row_var + EPS) * gain_bias[0:1, :] + gain_bias[1:2, :]).astype(BF)


def attend(x, wait, project, share, score, v_ref, w_out, bias, s_ref, step):
    rows = x.shape[0]
    heads = share // HD
    pages, page_len = v_ref.shape[:2]
    span = step * page_len
    scale = math.log2(math.e) / math.sqrt(HD)
    query, fresh_key, fresh_value = (project(x, i).astype(BF) for i in range(3))
    lane_head = lax.broadcasted_iota(jnp.int32, (rows, share), 1) // HD
    wide = jnp.concatenate(
        [jnp.where(lane_head == h, query.astype(F32), 0.0) for h in range(heads)], axis=0
    )
    own_key = jnp.concatenate([fresh_key.astype(F32)] * heads, axis=0)
    own = jnp.sum(wide * own_key, axis=-1, keepdims=True)
    wide = wide.astype(BF)
    peak = jnp.full((heads * rows, HD), -jnp.inf, F32)
    for c in range(pages // step):
        scores = score(wide, slice(c * span, (c + 1) * span))
        here = bias[:, c * span : (c + 1) * span]
        scores = scores + jnp.concatenate([here] * heads, axis=0)
        s_ref[:, c * span : (c + 1) * span] = scores
        for i in range(span // HD):
            peak = jnp.maximum(peak, scores[:, i * HD : (i + 1) * HD])
    peak = jnp.maximum(jnp.max(peak, axis=-1, keepdims=True), own)
    sums = jnp.zeros((heads * rows, HD), F32)
    mixed = jnp.zeros((heads * rows, share), F32)
    for c in range(pages // step):
        weight = jnp.exp2((s_ref[:, c * span : (c + 1) * span] - peak) * scale)
        for i in range(span // HD):
            sums = sums + weight[:, i * HD : (i + 1) * HD]
        wait("value", c * step)
        values = v_ref[c * step : (c + 1) * step].reshape(span, share)
        mixed = mixed + jnp.dot(weight.astype(BF), values, preferred_element_type=F32)
    own_weight = jnp.exp2((own - peak) * scale)
    total = jnp.sum(sums, axis=-1, keepdims=True) + own_weight
    fresh_value = fresh_value.astype(F32)
    own_weight = own_weight.astype(BF).astype(F32)
    attended = []
    for h in range(heads):
        r = slice(h * rows, (h + 1) * rows)
        f = slice(h * HD, (h + 1) * HD)
        attended.append((mixed[r, f] + own_weight[r] * fresh_value[:, f]) / total[r])
    attended = jnp.concatenate(attended, axis=1).astype(BF)
    return jnp.dot(attended, w_out[...], preferred_element_type=F32).astype(BF)


def k_step(pages):
    return math.gcd(pages, 21)


def score_scratch(rows, pages, page_len, share):
    return pltpu.VMEM((rows * share // HD, pages * page_len), F32)


def load(after, *sources):
    count = len(sources)

    def body(*refs):
        copies = [
            pltpu.make_async_copy(
                refs[1 + i] if layer is None else refs[1 + i].at[layer], refs[1 + count + i], refs[-1].at[i]
            )
            for i, (_, layer) in enumerate(sources)
        ]
        for copy in copies:
            copy.start()
        for copy in copies:
            copy.wait()

    shapes = [a.shape if layer is None else a.shape[1:] for a, layer in sources]
    return pl.pallas_call(
        body,
        out_shape=tuple(pltpu.VMEM(shape, BF) for shape in shapes),
        in_specs=[HBM_SPEC] * (1 + count),
        out_specs=(VMEM_SPEC,) * count,
        scratch_shapes=[pltpu.SemaphoreType.DMA((count,))],
        compiler_params=pltpu.CompilerParams(vmem_limit_bytes=MIB),
        cost_estimate=load_cost(shapes),
    )(after, *(in_place(a) for a, _ in sources))


def load_cost(shapes):
    size = sum(2 * math.prod(shape) for shape in shapes)
    return pl.CostEstimate(flops=0, transcendentals=0, bytes_accessed=2 * size)


def load_turned(after, key_cache, layer):
    pages, page_len, share = key_cache.shape[1:]
    step = math.gcd(pages, 14)
    parts = pages // step
    span = step * page_len

    def body(after_ref, k_hbm, out_ref, k_ref, sems):
        copies = [
            pltpu.make_async_copy(k_hbm.at[layer, pl.ds(c * step, step)], k_ref.at[pl.ds(c * step, step)], sems.at[c])
            for c in range(parts)
        ]
        for copy in copies[:3]:
            copy.start()
        for c in range(parts):
            copies[c].wait()
            if c + 3 < parts:
                copies[c + 3].start()
            keys = k_ref[c * step : (c + 1) * step].reshape(span, share)
            out_ref[:, c * span : (c + 1) * span] = jnp.transpose(keys)

    return pl.pallas_call(
        body,
        out_shape=pltpu.VMEM((share, pages * page_len), BF),
        in_specs=[HBM_SPEC] * 2,
        out_specs=VMEM_SPEC,
        scratch_shapes=[pltpu.VMEM((pages, page_len, share), BF), pltpu.SemaphoreType.DMA((parts,))],
        compiler_params=pltpu.CompilerParams(vmem_limit_bytes=10 * MIB),
        cost_estimate=load_cost([key_cache.shape[1:]]),
    )(after, in_place(key_cache))


def first_attention(incoming, take, w_qkv, w_out, key_cache, value_cache, bias):
    rows = bias.shape[0]
    lines, share = incoming.shape
    cols = take.shape[0] // rows

    pages, page_len = key_cache.shape[1:3]
    step = k_step(pages)
    parts = pages // step
    piece = w_qkv.shape[1] // SPLIT

    def body(in_ref, take_ref, b_ref, wo_ref, wq_hbm, k_hbm, v_hbm, x_ref, out_ref, wq_ref,
             s_ref, k_ref, v_ref, k_sems, v_sems, w_sems):
        copies = {}
        for i in range(3):
            for c in range(SPLIT):
                at = pl.ds(c * piece, piece)
                copies["qkv", i, c] = pltpu.make_async_copy(
                    wq_hbm.at[i, at], wq_ref.at[i, at], w_sems.at[i * SPLIT + c]
                )
        for c in range(parts):
            at = pl.ds(c * step, step)
            copies["key", c * step] = pltpu.make_async_copy(k_hbm.at[0, at], k_ref.at[at], k_sems.at[c])
        for c in range(parts):
            at = pl.ds(c * step, step)
            copies["value", c * step] = pltpu.make_async_copy(v_hbm.at[0, at], v_ref.at[at], v_sems.at[c])
        order = list(copies)
        for key in order[:DEPTH]:
            copies[key].start()

        def wait(*key):
            if key not in copies:
                return
            copies[key].wait()
            later = order.index(key) + DEPTH
            if later < len(order):
                copies[order[later]].start()

        def score(wide, at):
            wait("key", at.start // page_len)
            keys = k_ref[at.start // page_len : at.stop // page_len].reshape(at.stop - at.start, share)
            return lax.dot_general(wide, keys, (((1,), (1,)), ((), ())), preferred_element_type=F32)

        def project(x, i):
            total = None
            for c in range(SPLIT):
                wait("qkv", i, c)
                at = slice(c * piece, (c + 1) * piece)
                term = jnp.dot(x[:, at], wq_ref[i, at], preferred_element_type=F32)
                total = term if total is None else total + term
            return total

        stacked = jnp.dot(take_ref[...], in_ref[...], preferred_element_type=F32).astype(BF)
        x = jnp.concatenate([stacked[c * rows : (c + 1) * rows] for c in range(cols)], axis=1)
        x_ref[...] = x
        out_ref[...] = attend(x, wait, project, share, score, v_ref, wo_ref, b_ref, s_ref, math.gcd(step, STEP))

    shape = jax.ShapeDtypeStruct((rows, share * cols), BF)
    return pl.pallas_call(
        body,
        out_shape=(shape, shape, pltpu.VMEM(w_qkv.shape, BF)),
        in_specs=[VMEM_SPEC] * 4 + [HBM_SPEC] * 3,
        out_specs=(VMEM_SPEC,) * 3,
        scratch_shapes=[
            score_scratch(rows, pages, page_len, share),
            pltpu.VMEM(key_cache.shape[1:], BF),
            pltpu.VMEM(value_cache.shape[1:], BF),
            pltpu.SemaphoreType.DMA((parts,)),
            pltpu.SemaphoreType.DMA((parts,)),
            pltpu.SemaphoreType.DMA((3 * SPLIT,)),
        ],
        compiler_params=pltpu.CompilerParams(vmem_limit_bytes=24 * MIB),
    )(incoming, take, bias, w_out, *map(in_place, (w_qkv, key_cache, value_cache)))


def norm_attention(parts, residual, gain_bias, w_qkv, w_out, keys, values, bias):
    count = len(parts)
    step = math.gcd(values.shape[0], 6)

    def body(*refs):
        part_refs, (res_ref, norm_ref, wq_ref, wo_ref, k_ref, v_ref, b_ref) = refs[:count], refs[count : count + 7]
        x_ref, out_ref, s_ref = refs[count + 7 :]
        x = add_norm([r[...] for r in part_refs], res_ref[...], norm_ref[...])
        x_ref[...] = x

        def score(wide, at):
            return jnp.dot(wide, k_ref[:, at], preferred_element_type=F32)

        def project(x, i):
            return jnp.dot(x, wq_ref[i], preferred_element_type=F32)

        out_ref[...] = attend(x, lambda *key: None, project, wq_ref.shape[2], score, v_ref, wo_ref, b_ref, s_ref, step)

    shape = jax.ShapeDtypeStruct(residual.shape, BF)
    scratch = [score_scratch(residual.shape[0], *values.shape)]
    return kernel_call(
        body, (shape, shape), scratch, 12, *parts, residual, gain_bias, w_qkv, w_out, keys, values, bias
    )


def norm_mlp(parts, residual, gain_bias, w_up, w_down):
    count = len(parts)

    def body(*refs):
        part_refs, (res_ref, norm_ref, up_ref, down_ref) = refs[:count], refs[count : count + 4]
        x_ref, out_ref = refs[count + 4 :]
        x = add_norm([r[...] for r in part_refs], res_ref[...], norm_ref[...])
        x_ref[...] = x
        up = jnp.dot(x, up_ref[...], preferred_element_type=F32)
        active = jax.nn.gelu(up, approximate=True).astype(BF)
        out_ref[...] = jnp.dot(active, down_ref[...], preferred_element_type=F32).astype(BF)

    shape = jax.ShapeDtypeStruct(residual.shape, BF)
    return kernel_call(body, (shape, shape), [], 8, *parts, residual, gain_bias, w_up, w_down)


def norm_send(parts, residual, gain_bias, give):
    count = len(parts)
    cols = give.shape[1] // residual.shape[0]
    share = residual.shape[1] // cols

    def body(*refs):
        res_ref, norm_ref, give_ref, out_ref = refs[count:]
        x = add_norm([r[...] for r in refs[:count]], res_ref[...], norm_ref[...])
        out_ref[...] = lay_out(give_ref[...], x, cols)

    shape = jax.ShapeDtypeStruct((give.shape[0], share), BF)
    return kernel_call(body, shape, [], 8, *parts, residual, gain_bias, give)


def lay_out(give, rows_here, cols):
    share = rows_here.shape[1] // cols
    stacked = jnp.concatenate([rows_here[:, c * share : (c + 1) * share] for c in range(cols)], axis=0)
    return jnp.dot(give, stacked, preferred_element_type=F32).astype(BF)


def gather_parts(part):
    size = lax.axis_size("tp")
    return [part] + [
        lax.ppermute(part, "tp", [(i, (i + step) % size) for i in range(size)])
        for step in range(size - 1, 0, -1)
    ]


def iota(shape, dim):
    return lax.broadcasted_iota(jnp.int32, shape, dim)


def deal_send(order, tokens, blocks, cols):
    rows, width = tokens.shape
    lines, stack = blocks * CAP * cols, cols * rows
    groups, lanes = order.shape
    near = lanes // rows * CAP * cols

    def body(order_hbm, tok_hbm, out_ref, back_ref, order_ref, tok_ref, sems):
        order_copy = pltpu.make_async_copy(order_hbm, order_ref, sems.at[0])
        token_copy = pltpu.make_async_copy(tok_hbm, tok_ref, sems.at[1])
        order_copy.start()
        token_copy.start()
        wanted = lax.axis_index("req") * rows + iota((rows, lanes), 0)
        spread = iota((lanes, lines), 0) // rows == iota((lanes, lines), 1) % near // (CAP * cols)
        spread = spread.astype(F32).astype(BF)
        line = iota((rows, lines), 1)
        earlier = (iota((rows, rows), 1) < iota((rows, rows), 0)).astype(F32).astype(BF)
        order_copy.wait()
        goes = jnp.concatenate(
            [(order_ref[r : r + 1, :] == wanted).astype(F32).astype(BF) for r in range(groups)], axis=0
        )
        sent_by_group = jnp.dot(goes, spread, preferred_element_type=F32)
        sent = jnp.zeros((rows, lines), F32)
        for r in range(groups):
            sent = jnp.where(line // near == r, sent_by_group[r * rows : (r + 1) * rows], sent)
        rank = jnp.dot(earlier, sent.astype(BF), preferred_element_type=F32).astype(jnp.int32)
        mine = jnp.where(rank == line // cols % CAP, sent, 0.0)
        back = jnp.concatenate([jnp.where(line % cols == c, mine, 0.0) for c in range(cols)], axis=0)
        back_ref[...] = back.astype(BF)
        token_copy.wait()
        out_ref[...] = lay_out(jnp.transpose(back).astype(BF), tok_ref[...], cols)

    return pl.pallas_call(
        body,
        out_shape=(
            jax.ShapeDtypeStruct((lines, width // cols), BF),
            jax.ShapeDtypeStruct((stack, lines), BF),
        ),
        in_specs=[HBM_SPEC] * 2,
        out_specs=(VMEM_SPEC,) * 2,
        scratch_shapes=[
            pltpu.VMEM(order.shape, order.dtype),
            pltpu.VMEM(tokens.shape, BF),
            pltpu.SemaphoreType.DMA((2,)),
        ],
        compiler_params=pltpu.CompilerParams(vmem_limit_bytes=8 * MIB),
    )(in_place(order), in_place(tokens))


def deal_take(order, table, lengths, w_out, blocks, cols, pages, page_len):
    rows = lengths.shape[1]
    lines, stack = blocks * CAP * cols, cols * rows

    def body(order_ref, table_ref, len_ref, wo_hbm, take_ref, send_ref, bias_ref, wo_ref, sem):
        copy = pltpu.make_async_copy(wo_hbm, wo_ref, sem)
        copy.start()
        req = lax.axis_index("req")
        slot = req * rows + iota((stack, order.shape[1]), 0) % rows
        mine = jnp.zeros((stack, order.shape[1]), F32)
        for r in range(order.shape[0]):
            here = iota((stack, order.shape[1]), 1) + r * order.shape[1]
            mine = mine + jnp.where(here == slot, order_ref[r : r + 1, :], 0).astype(F32)
        column = jnp.broadcast_to(jnp.sum(mine, axis=1, keepdims=True), (stack, stack))
        line_of = jnp.transpose(column).astype(jnp.int32)
        column = column.astype(jnp.int32)
        a, b = iota((stack, stack), 0), iota((stack, stack), 1)
        before = (b < rows) & (column // rows == line_of // rows) & (line_of < column)
        rank = jnp.sum(before.astype(F32), axis=1, keepdims=True).astype(jnp.int32)
        place = (column[:, 0:1] // rows * CAP + rank) * cols + iota((stack, 1), 0) // rows
        take = (iota((stack, lines), 1) == place).astype(F32)
        take_ref[...] = take.astype(BF)
        send_ref[...] = jnp.transpose(take).astype(BF)
        diagonal = iota((rows, rows), 0) == iota((rows, rows), 1)

        def stand(line):
            return jnp.sum(jnp.where(diagonal, line, 0).astype(F32), axis=1, keepdims=True).astype(jnp.int32)

        length = stand(len_ref[...])
        page = iota((rows, page_len), 1) + req * pages
        room = jnp.zeros((rows, page_len), jnp.int32)
        for k in range(table.shape[0]):
            left = length - k * page_len
            hit = (stand(table_ref[k : k + 1, :]) == page) & (left > 0)
            room = room + jnp.where(hit, left, 0)
        offset = iota((rows, page_len), 1)
        for p in range(pages):
            bias_ref[:, p * page_len : (p + 1) * page_len] = jnp.where(
                offset < room[:, p : p + 1], 0.0, -jnp.inf
            ).astype(F32)
        copy.wait()

    out = (
        jax.ShapeDtypeStruct((stack, lines), BF),
        jax.ShapeDtypeStruct((lines, stack), BF),
        jax.ShapeDtypeStruct((rows, pages * page_len), F32),
        pltpu.VMEM(w_out.shape, BF),
    )
    return pl.pallas_call(
        body,
        out_shape=out,
        in_specs=[VMEM_SPEC] * 3 + [HBM_SPEC],
        out_specs=(VMEM_SPEC,) * 4,
        scratch_shapes=[pltpu.SemaphoreType.DMA],
        compiler_params=pltpu.CompilerParams(vmem_limit_bytes=8 * MIB),
    )(order, table, lengths, in_place(w_out))


def settle(incoming, back, rows):
    cols = back.shape[0] // rows

    def body(in_ref, back_ref, out_ref):
        stacked = jnp.dot(back_ref[...], in_ref[...], preferred_element_type=F32).astype(BF)
        out_ref[...] = jnp.concatenate([stacked[c * rows : (c + 1) * rows] for c in range(cols)], axis=1)

    shape = jax.ShapeDtypeStruct((rows, incoming.shape[1] * cols), BF)
    return kernel_call(body, shape, [], 8, incoming, back)


def swap(lines_out, blocks):
    lines, share = lines_out.shape
    return lax.all_to_all(lines_out.reshape(blocks, lines // blocks, share), "req", 0, 0).reshape(lines, share)


def local(
    tokens,
    deal_order,
    page_table,
    lengths,
    qkv_weight,
    out_weight,
    up_weight,
    down_weight,
    key_cache,
    value_cache,
    attn_norm,
    mlp_norm,
):
    req_rows = tokens.shape[0]
    blocks = lax.axis_size("req")
    cols = lax.axis_size("tp")
    layers, pool_pages, page_len = key_cache.shape[:3]
    order = deal_order.reshape(-1, HD)
    outgoing, back = deal_send(order, tokens, blocks, cols)
    incoming = swap(outgoing, blocks)
    take, send, bias, w_out = deal_take(
        order, page_table.T, lengths.reshape(1, -1), out_weight, blocks, cols, pool_pages, page_len
    )
    w_qkv = jnp.transpose(qkv_weight, (1, 0, 2))
    current, partial, w_qkv = first_attention(incoming, take, w_qkv, w_out, key_cache, value_cache, bias)
    w_up, w_down, values = load(partial, (up_weight, None), (down_weight, None), (value_cache, 1))
    for layer in range(layers):
        hidden, partial = norm_mlp(gather_parts(partial), current, attn_norm, w_up, w_down)
        if layer + 1 < layers:
            keys = load_turned(partial, key_cache, layer + 1)
            current, partial = norm_attention(
                gather_parts(partial), hidden, mlp_norm, w_qkv, w_out, keys, values, bias
            )
            if layer + 2 < layers:
                (values,) = load(partial, (value_cache, layer + 2))
    leaving = norm_send(gather_parts(partial), hidden, mlp_norm, send)
    return settle(swap(leaving, blocks), back, req_rows)


def solution(mesh):
    in_specs = (
        P("req", None),
        P(),
        P("req", None),
        P("req"),
        P(None, None, "tp"),
        P("tp", None),
        P(None, "tp"),
        P("tp", None),
        P(None, "req", None, "tp"),
        P(None, "req", None, "tp"),
        P(),
        P(),
    )
    out_specs = P("req", None)
    return jax.shard_map(local, mesh=mesh, in_specs=in_specs, out_specs=out_specs, check_vma=False)
```

```python
import math

import jax
import jax.numpy as jnp
from jax import lax
from jax.experimental import pallas as pl
from jax.experimental.pallas import tpu as pltpu
from jax.sharding import PartitionSpec as P

HD = 128
CAP = 2
EPS = 1e-6
BF = jnp.bfloat16
F32 = jnp.float32
MIB = 1 << 20
DEPTH = 4
STEP = 7
SPLIT = 1
VMEM_SPEC = pl.BlockSpec(memory_space=pltpu.VMEM)
HBM_SPEC = pl.BlockSpec(memory_space=pltpu.HBM)


def kernel_call(body, out_shape, scratch, limit_mib, *operands):
    return pl.pallas_call(
        body,
        out_shape=out_shape,
        in_specs=[VMEM_SPEC] * len(operands),
        out_specs=jax.tree.map(lambda _: VMEM_SPEC, out_shape),
        scratch_shapes=scratch,
        compiler_params=pltpu.CompilerParams(vmem_limit_bytes=limit_mib * MIB),
    )(*operands)


def in_place(array):
    return pltpu.with_memory_space_constraint(array, pltpu.HBM)


def add_norm(parts, residual, gain_bias):
    total = residual.astype(F32)
    for part in parts:
        total = total + part.astype(F32)
    width = total.shape[-1]
    row_mean = jnp.sum(total, axis=-1, keepdims=True) * (1.0 / width)
    centered = total - row_mean
    row_var = jnp.sum(centered * centered, axis=-1, keepdims=True) * (1.0 / width)
    return (centered * lax.rsqrt(row_var + EPS) * gain_bias[0:1, :] + gain_bias[1:2, :]).astype(BF)


def attend(x, wait, project, share, score, pages, page_len, value, w_out, bias, s_ref, step):
    rows = x.shape[0]
    heads = share // HD
    span = step * page_len
    scale = math.log2(math.e) / math.sqrt(HD)
    query, fresh_key, fresh_value = (project(x, i).astype(BF) for i in range(3))
    lane_head = lax.broadcasted_iota(jnp.int32, (rows, share), 1) // HD
    wide = jnp.concatenate(
        [jnp.where(lane_head == h, query.astype(F32), 0.0) for h in range(heads)], axis=0
    )
    own_key = jnp.concatenate([fresh_key.astype(F32)] * heads, axis=0)
    own = jnp.sum(wide * own_key, axis=-1, keepdims=True)
    wide = wide.astype(BF)
    peak = jnp.full((heads * rows, HD), -jnp.inf, F32)
    for c in range(pages // step):
        scores = score(wide, slice(c * span, (c + 1) * span))
        here = bias[:, c * span : (c + 1) * span]
        scores = scores + jnp.concatenate([here] * heads, axis=0)
        s_ref[:, c * span : (c + 1) * span] = scores
        for i in range(span // HD):
            peak = jnp.maximum(peak, scores[:, i * HD : (i + 1) * HD])
    peak = jnp.maximum(jnp.max(peak, axis=-1, keepdims=True), own)
    sums = jnp.zeros((heads * rows, HD), F32)
    mixed = jnp.zeros((heads * rows, share), F32)
    for c in range(pages // step):
        weight = jnp.exp2((s_ref[:, c * span : (c + 1) * span] - peak) * scale)
        for i in range(span // HD):
            sums = sums + weight[:, i * HD : (i + 1) * HD]
        wait("value", c * step)
        values = value(c * step, step).reshape(span, share)
        mixed = mixed + jnp.dot(weight.astype(BF), values, preferred_element_type=F32)
    own_weight = jnp.exp2((own - peak) * scale)
    total = jnp.sum(sums, axis=-1, keepdims=True) + own_weight
    fresh_value = fresh_value.astype(F32)
    own_weight = own_weight.astype(BF).astype(F32)
    attended = []
    for h in range(heads):
        r = slice(h * rows, (h + 1) * rows)
        f = slice(h * HD, (h + 1) * HD)
        attended.append((mixed[r, f] + own_weight[r] * fresh_value[:, f]) / total[r])
    attended = jnp.concatenate(attended, axis=1).astype(BF)
    return jnp.dot(attended, w_out[...], preferred_element_type=F32).astype(BF)


def k_step(pages):
    return math.gcd(pages, 21)


def score_scratch(rows, pages, page_len, share):
    return pltpu.VMEM((rows * share // HD, pages * page_len), F32)


def load(after, *sources):
    count = len(sources)

    def body(*refs):
        copies = [
            pltpu.make_async_copy(
                refs[1 + i] if at is None else refs[1 + i].at[at[0], pl.ds(0, at[1])], refs[1 + count + i], refs[-1].at[i]
            )
            for i, (_, at) in enumerate(sources)
        ]
        for copy in copies:
            copy.start()
        for copy in copies:
            copy.wait()

    shapes = [a.shape if at is None else (at[1], *a.shape[2:]) for a, at in sources]
    return pl.pallas_call(
        body,
        out_shape=tuple(pltpu.VMEM(shape, BF) for shape in shapes),
        in_specs=[HBM_SPEC] * (1 + count),
        out_specs=(VMEM_SPEC,) * count,
        scratch_shapes=[pltpu.SemaphoreType.DMA((count,))],
        compiler_params=pltpu.CompilerParams(vmem_limit_bytes=MIB),
        cost_estimate=load_cost(shapes),
    )(after, *(in_place(a) for a, _ in sources))


def load_cost(shapes):
    size = sum(2 * math.prod(shape) for shape in shapes)
    return pl.CostEstimate(flops=0, transcendentals=0, bytes_accessed=2 * size)


def load_turned(after, key_cache, value_cache, layer, cut):
    pages, page_len, share = key_cache.shape[1:]
    step = math.gcd(pages, 14)
    parts = pages // step
    span = step * page_len

    def body(after_ref, k_hbm, v_hbm, out_ref, late_ref, k_ref, sems):
        late = pltpu.make_async_copy(v_hbm.at[layer, pl.ds(cut, pages - cut)], late_ref, sems.at[parts])
        copies = [
            pltpu.make_async_copy(k_hbm.at[layer, pl.ds(c * step, step)], k_ref.at[pl.ds(c * step, step)], sems.at[c])
            for c in range(parts)
        ]
        for copy in copies[:3]:
            copy.start()
        for c in range(parts):
            copies[c].wait()
            if c + 3 < parts:
                copies[c + 3].start()
            if c == 0:
                late.start()
            keys = k_ref[c * step : (c + 1) * step].reshape(span, share)
            out_ref[:, c * span : (c + 1) * span] = jnp.transpose(keys)
        late.wait()

    return pl.pallas_call(
        body,
        out_shape=(pltpu.VMEM((share, pages * page_len), BF), pltpu.VMEM((pages - cut, page_len, share), BF)),
        in_specs=[HBM_SPEC] * 3,
        out_specs=(VMEM_SPEC,) * 2,
        scratch_shapes=[pltpu.VMEM((pages, page_len, share), BF), pltpu.SemaphoreType.DMA((parts + 1,))],
        compiler_params=pltpu.CompilerParams(vmem_limit_bytes=10 * MIB),
        cost_estimate=load_cost([key_cache.shape[1:]]),
    )(after, in_place(key_cache), in_place(value_cache))


def first_attention(incoming, take, w_qkv, w_out, key_cache, value_cache, bias):
    rows = bias.shape[0]
    lines, share = incoming.shape
    cols = take.shape[0] // rows

    pages, page_len = key_cache.shape[1:3]
    step = k_step(pages)
    parts = pages // step
    piece = w_qkv.shape[1] // SPLIT

    def body(in_ref, take_ref, b_ref, wo_ref, wq_hbm, k_hbm, v_hbm, x_ref, out_ref, wq_ref,
             s_ref, k_ref, v_ref, k_sems, v_sems, w_sems):
        copies = {}
        for i in range(3):
            for c in range(SPLIT):
                at = pl.ds(c * piece, piece)
                copies["qkv", i, c] = pltpu.make_async_copy(
                    wq_hbm.at[i, at], wq_ref.at[i, at], w_sems.at[i * SPLIT + c]
                )
        for c in range(parts):
            at = pl.ds(c * step, step)
            copies["key", c * step] = pltpu.make_async_copy(k_hbm.at[0, at], k_ref.at[at], k_sems.at[c])
        for c in range(parts):
            at = pl.ds(c * step, step)
            copies["value", c * step] = pltpu.make_async_copy(v_hbm.at[0, at], v_ref.at[at], v_sems.at[c])
        order = list(copies)
        for key in order[:DEPTH]:
            copies[key].start()

        def wait(*key):
            if key not in copies:
                return
            copies[key].wait()
            later = order.index(key) + DEPTH
            if later < len(order):
                copies[order[later]].start()

        def score(wide, at):
            wait("key", at.start // page_len)
            keys = k_ref[at.start // page_len : at.stop // page_len].reshape(at.stop - at.start, share)
            return lax.dot_general(wide, keys, (((1,), (1,)), ((), ())), preferred_element_type=F32)

        def project(x, i):
            total = None
            for c in range(SPLIT):
                wait("qkv", i, c)
                at = slice(c * piece, (c + 1) * piece)
                term = jnp.dot(x[:, at], wq_ref[i, at], preferred_element_type=F32)
                total = term if total is None else total + term
            return total

        stacked = jnp.dot(take_ref[...], in_ref[...], preferred_element_type=F32).astype(BF)
        x = jnp.concatenate([stacked[c * rows : (c + 1) * rows] for c in range(cols)], axis=1)
        x_ref[...] = x
        def value(first, count):
            return v_ref[first : first + count]

        out_ref[...] = attend(
            x, wait, project, share, score, pages, page_len, value, wo_ref, b_ref, s_ref, math.gcd(step, STEP)
        )

    shape = jax.ShapeDtypeStruct((rows, share * cols), BF)
    return pl.pallas_call(
        body,
        out_shape=(shape, shape, pltpu.VMEM(w_qkv.shape, BF)),
        in_specs=[VMEM_SPEC] * 4 + [HBM_SPEC] * 3,
        out_specs=(VMEM_SPEC,) * 3,
        scratch_shapes=[
            score_scratch(rows, pages, page_len, share),
            pltpu.VMEM(key_cache.shape[1:], BF),
            pltpu.VMEM(value_cache.shape[1:], BF),
            pltpu.SemaphoreType.DMA((parts,)),
            pltpu.SemaphoreType.DMA((parts,)),
            pltpu.SemaphoreType.DMA((3 * SPLIT,)),
        ],
        compiler_params=pltpu.CompilerParams(vmem_limit_bytes=24 * MIB),
    )(incoming, take, bias, w_out, *map(in_place, (w_qkv, key_cache, value_cache)))


def norm_attention(parts, residual, gain_bias, w_qkv, w_out, keys, early, late, bias):
    count = len(parts)
    cut, page_len, share = early.shape
    pages = cut + late.shape[0]
    step = math.gcd(cut, late.shape[0])

    def body(*refs):
        part_refs, (res_ref, norm_ref, wq_ref, wo_ref, k_ref, v0_ref, v1_ref, b_ref) = refs[:count], refs[count : count + 8]
        x_ref, out_ref, s_ref = refs[count + 8 :]
        x = add_norm([r[...] for r in part_refs], res_ref[...], norm_ref[...])
        x_ref[...] = x

        def score(wide, at):
            return jnp.dot(wide, k_ref[:, at], preferred_element_type=F32)

        def project(x, i):
            return jnp.dot(x, wq_ref[i], preferred_element_type=F32)

        def value(first, number):
            if first < cut:
                return v0_ref[first : first + number]
            return v1_ref[first - cut : first - cut + number]

        out_ref[...] = attend(
            x, lambda *key: None, project, share, score, pages, page_len, value, wo_ref, b_ref, s_ref, step
        )

    shape = jax.ShapeDtypeStruct(residual.shape, BF)
    scratch = [score_scratch(residual.shape[0], pages, page_len, share)]
    return kernel_call(
        body, (shape, shape), scratch, 12, *parts, residual, gain_bias, w_qkv, w_out, keys, early, late, bias
    )


def norm_mlp(parts, residual, gain_bias, w_up, w_down):
    count = len(parts)

    def body(*refs):
        part_refs, (res_ref, norm_ref, up_ref, down_ref) = refs[:count], refs[count : count + 4]
        x_ref, out_ref = refs[count + 4 :]
        x = add_norm([r[...] for r in part_refs], res_ref[...], norm_ref[...])
        x_ref[...] = x
        up = jnp.dot(x, up_ref[...], preferred_element_type=F32)
        active = jax.nn.gelu(up, approximate=True).astype(BF)
        out_ref[...] = jnp.dot(active, down_ref[...], preferred_element_type=F32).astype(BF)

    shape = jax.ShapeDtypeStruct(residual.shape, BF)
    return kernel_call(body, (shape, shape), [], 8, *parts, residual, gain_bias, w_up, w_down)


def norm_send(parts, residual, gain_bias, give):
    count = len(parts)
    cols = give.shape[1] // residual.shape[0]
    share = residual.shape[1] // cols

    def body(*refs):
        res_ref, norm_ref, give_ref, out_ref = refs[count:]
        x = add_norm([r[...] for r in refs[:count]], res_ref[...], norm_ref[...])
        out_ref[...] = lay_out(give_ref[...], x, cols)

    shape = jax.ShapeDtypeStruct((give.shape[0], share), BF)
    return kernel_call(body, shape, [], 8, *parts, residual, gain_bias, give)


def lay_out(give, rows_here, cols):
    share = rows_here.shape[1] // cols
    stacked = jnp.concatenate([rows_here[:, c * share : (c + 1) * share] for c in range(cols)], axis=0)
    return jnp.dot(give, stacked, preferred_element_type=F32).astype(BF)


def gather_parts(part):
    size = lax.axis_size("tp")
    return [part] + [
        lax.ppermute(part, "tp", [(i, (i + step) % size) for i in range(size)])
        for step in range(size - 1, 0, -1)
    ]


def iota(shape, dim):
    return lax.broadcasted_iota(jnp.int32, shape, dim)


def deal_send(order, tokens, blocks, cols):
    rows, width = tokens.shape
    lines, stack = blocks * CAP * cols, cols * rows
    groups, lanes = order.shape
    near = lanes // rows * CAP * cols

    def body(order_hbm, tok_hbm, out_ref, back_ref, order_ref, tok_ref, sems):
        order_copy = pltpu.make_async_copy(order_hbm, order_ref, sems.at[0])
        token_copy = pltpu.make_async_copy(tok_hbm, tok_ref, sems.at[1])
        order_copy.start()
        token_copy.start()
        wanted = lax.axis_index("req") * rows + iota((rows, lanes), 0)
        spread = iota((lanes, lines), 0) // rows == iota((lanes, lines), 1) % near // (CAP * cols)
        spread = spread.astype(F32).astype(BF)
        line = iota((rows, lines), 1)
        earlier = (iota((rows, rows), 1) < iota((rows, rows), 0)).astype(F32).astype(BF)
        order_copy.wait()
        goes = jnp.concatenate(
            [(order_ref[r : r + 1, :] == wanted).astype(F32).astype(BF) for r in range(groups)], axis=0
        )
        sent_by_group = jnp.dot(goes, spread, preferred_element_type=F32)
        sent = jnp.zeros((rows, lines), F32)
        for r in range(groups):
            sent = jnp.where(line // near == r, sent_by_group[r * rows : (r + 1) * rows], sent)
        rank = jnp.dot(earlier, sent.astype(BF), preferred_element_type=F32).astype(jnp.int32)
        mine = jnp.where(rank == line // cols % CAP, sent, 0.0)
        back = jnp.concatenate([jnp.where(line % cols == c, mine, 0.0) for c in range(cols)], axis=0)
        back_ref[...] = back.astype(BF)
        token_copy.wait()
        out_ref[...] = lay_out(jnp.transpose(back).astype(BF), tok_ref[...], cols)

    return pl.pallas_call(
        body,
        out_shape=(
            jax.ShapeDtypeStruct((lines, width // cols), BF),
            jax.ShapeDtypeStruct((stack, lines), BF),
        ),
        in_specs=[HBM_SPEC] * 2,
        out_specs=(VMEM_SPEC,) * 2,
        scratch_shapes=[
            pltpu.VMEM(order.shape, order.dtype),
            pltpu.VMEM(tokens.shape, BF),
            pltpu.SemaphoreType.DMA((2,)),
        ],
        compiler_params=pltpu.CompilerParams(vmem_limit_bytes=8 * MIB),
    )(in_place(order), in_place(tokens))


def deal_take(order, table, lengths, w_out, blocks, cols, pages, page_len):
    rows = lengths.shape[1]
    lines, stack = blocks * CAP * cols, cols * rows

    def body(order_ref, table_ref, len_ref, wo_hbm, take_ref, send_ref, bias_ref, wo_ref, sem):
        copy = pltpu.make_async_copy(wo_hbm, wo_ref, sem)
        copy.start()
        req = lax.axis_index("req")
        slot = req * rows + iota((stack, order.shape[1]), 0) % rows
        mine = jnp.zeros((stack, order.shape[1]), F32)
        for r in range(order.shape[0]):
            here = iota((stack, order.shape[1]), 1) + r * order.shape[1]
            mine = mine + jnp.where(here == slot, order_ref[r : r + 1, :], 0).astype(F32)
        column = jnp.broadcast_to(jnp.sum(mine, axis=1, keepdims=True), (stack, stack))
        line_of = jnp.transpose(column).astype(jnp.int32)
        column = column.astype(jnp.int32)
        a, b = iota((stack, stack), 0), iota((stack, stack), 1)
        before = (b < rows) & (column // rows == line_of // rows) & (line_of < column)
        rank = jnp.sum(before.astype(F32), axis=1, keepdims=True).astype(jnp.int32)
        place = (column[:, 0:1] // rows * CAP + rank) * cols + iota((stack, 1), 0) // rows
        take = (iota((stack, lines), 1) == place).astype(F32)
        take_ref[...] = take.astype(BF)
        send_ref[...] = jnp.transpose(take).astype(BF)
        diagonal = iota((rows, rows), 0) == iota((rows, rows), 1)

        def stand(line):
            return jnp.sum(jnp.where(diagonal, line, 0).astype(F32), axis=1, keepdims=True).astype(jnp.int32)

        length = stand(len_ref[...])
        page = iota((rows, page_len), 1) + req * pages
        room = jnp.zeros((rows, page_len), jnp.int32)
        for k in range(table.shape[0]):
            left = length - k * page_len
            hit = (stand(table_ref[k : k + 1, :]) == page) & (left > 0)
            room = room + jnp.where(hit, left, 0)
        offset = iota((rows, page_len), 1)
        for p in range(pages):
            bias_ref[:, p * page_len : (p + 1) * page_len] = jnp.where(
                offset < room[:, p : p + 1], 0.0, -jnp.inf
            ).astype(F32)
        copy.wait()

    out = (
        jax.ShapeDtypeStruct((stack, lines), BF),
        jax.ShapeDtypeStruct((lines, stack), BF),
        jax.ShapeDtypeStruct((rows, pages * page_len), F32),
        pltpu.VMEM(w_out.shape, BF),
    )
    return pl.pallas_call(
        body,
        out_shape=out,
        in_specs=[VMEM_SPEC] * 3 + [HBM_SPEC],
        out_specs=(VMEM_SPEC,) * 4,
        scratch_shapes=[pltpu.SemaphoreType.DMA],
        compiler_params=pltpu.CompilerParams(vmem_limit_bytes=8 * MIB),
    )(order, table, lengths, in_place(w_out))


def settle(incoming, back, rows):
    cols = back.shape[0] // rows

    def body(in_ref, back_ref, out_ref):
        stacked = jnp.dot(back_ref[...], in_ref[...], preferred_element_type=F32).astype(BF)
        out_ref[...] = jnp.concatenate([stacked[c * rows : (c + 1) * rows] for c in range(cols)], axis=1)

    shape = jax.ShapeDtypeStruct((rows, incoming.shape[1] * cols), BF)
    return kernel_call(body, shape, [], 8, incoming, back)


def swap(lines_out, blocks):
    lines, share = lines_out.shape
    return lax.all_to_all(lines_out.reshape(blocks, lines // blocks, share), "req", 0, 0).reshape(lines, share)


def local(
    tokens,
    deal_order,
    page_table,
    lengths,
    qkv_weight,
    out_weight,
    up_weight,
    down_weight,
    key_cache,
    value_cache,
    attn_norm,
    mlp_norm,
):
    req_rows = tokens.shape[0]
    blocks = lax.axis_size("req")
    cols = lax.axis_size("tp")
    layers, pool_pages, page_len = key_cache.shape[:3]
    order = deal_order.reshape(-1, HD)
    outgoing, back = deal_send(order, tokens, blocks, cols)
    incoming = swap(outgoing, blocks)
    take, send, bias, w_out = deal_take(
        order, page_table.T, lengths.reshape(1, -1), out_weight, blocks, cols, pool_pages, page_len
    )
    w_qkv = jnp.transpose(qkv_weight, (1, 0, 2))
    current, partial, w_qkv = first_attention(incoming, take, w_qkv, w_out, key_cache, value_cache, bias)
    cut = pool_pages * 4 // 7
    w_up, w_down, early = load(partial, (up_weight, None), (down_weight, None), (value_cache, (1, cut)))
    for layer in range(layers):
        hidden, partial = norm_mlp(gather_parts(partial), current, attn_norm, w_up, w_down)
        if layer + 1 < layers:
            keys, late = load_turned(partial, key_cache, value_cache, layer + 1, cut)
            current, partial = norm_attention(
                gather_parts(partial), hidden, mlp_norm, w_qkv, w_out, keys, early, late, bias
            )
            if layer + 2 < layers:
                (early,) = load(partial, (value_cache, (layer + 2, cut)))
    leaving = norm_send(gather_parts(partial), hidden, mlp_norm, send)
    return settle(swap(leaving, blocks), back, req_rows)


def solution(mesh):
    in_specs = (
        P("req", None),
        P(),
        P("req", None),
        P("req"),
        P(None, None, "tp"),
        P("tp", None),
        P(None, "tp"),
        P("tp", None),
        P(None, "req", None, "tp"),
        P(None, "req", None, "tp"),
        P(),
        P(),
    )
    out_specs = P("req", None)
    return jax.shard_map(local, mesh=mesh, in_specs=in_specs, out_specs=out_specs, check_vma=False)
```
